32 devices in a mesh: rows: 8 (over z, y), cols: 4 (over x, core).
Axes of the slice: x: 2, y: 2, z: 4, core: 2. Of those that a mesh axis runs over, the one named last changes fastest.
Arguments:
- feats_t: bfloat16 [128, 16384], P('cols', 'rows'), may hold values from -6 to 6
- adj_index: int32 [128, 16], replicated, may hold values from 0 to 127, as said below
- adj_weight: bfloat16 [128, 16, 128, 128], P('rows'), as said below
- weight: bfloat16 [128, 256], replicated, may hold values from -0.5 to 0.5
- cotangent_t: bfloat16 [256, 16384], P('cols', 'rows'), may hold values from -6 to 6
Outputs:
- output_t: bfloat16 [256, 16384], P('cols', 'rows')
- weight_grad: float32 [128, 256], P('cols')
- feat_grad: float32 [128, 16384], P('cols', 'rows')
The draws below stay inside these ranges and needn't reach their ends.
Inputs may be any that keep to these rules, and one draw needn't show every extreme that they name: `adj_index`: slot 0 of row block i names block i itself. Blocks are grouped 16 to a device in order. Slot 1 names a block of the next device (device index plus one, cyclically). The row blocks of one device name at most 4 distinct blocks of any other device, and exactly 4 of the next one. A block may stand in several slots of one row block. `adj_weight`: Nonnegative; about one entry in eight is nonzero.
All inputs are finite; a program needn't handle non-finite values.
Results may differ from the reference program's by a relative error of at most 0.0054.
Values may be sent and summed in bfloat16 or wider, within the bound.
No kernel may reach another device: no remote copies, remote signals or barrier semaphores. Data moves between devices by JAX's collectives and lax.ppermute only.
A program may use at most 128 MiB of HBM per device.

```python
import jax
import jax.numpy as jnp
from jax import lax

F_IN = 128
UNITS = 256
TILE = 128
KB = 16
BLK_DEV = 16
CAP = 4
NB = 128
NODES = 16384


def draw_adj_index(key, part):
    row_devs = NB // BLK_DEV
    key_sub, key_src, key_pick = jax.random.split(jax.random.fold_in(key, 11), 3)
    scores = jax.random.randint(key_sub, (row_devs, row_devs, BLK_DEV), 0, 2 ** 20) * BLK_DEV + jnp.arange(BLK_DEV, dtype=jnp.int32)
    subset = lax.top_k(scores, CAP)[1].astype(jnp.int32)
    blocks = jnp.arange(NB, dtype=jnp.int32)
    owner = blocks // BLK_DEV
    within = blocks % BLK_DEV
    after = (owner + 1) % row_devs
    first = after * BLK_DEV + subset[owner, after, within % CAP]
    offsets = jax.random.randint(key_src, (NB, KB - 2), 1, row_devs)
    source = (owner[:, None] + offsets) % row_devs
    choose = jax.random.randint(key_pick, (NB, KB - 2), 0, CAP)
    others = source * BLK_DEV + subset[owner[:, None], source, choose]
    return jnp.concatenate([blocks[:, None], first[:, None], others], axis=1).astype(jnp.int32)


def draw_adj_weight(key, part):
    key_mask, key_val = jax.random.split(jax.random.fold_in(key, 23))
    shape = (NB, KB, TILE, TILE)
    present = (jax.random.uniform(key_mask, shape) < 0.125).astype(jnp.float32)
    values = jax.random.uniform(key_val, shape, minval=0.5, maxval=1.5)
    norm = 1.0 / jnp.sqrt(jnp.float32(KB * TILE) / 8.0)
    return (present * values * norm).astype(jnp.bfloat16)


def level_of(own_key, dims, pieces, low, high):
    gain, own = 1.0, jax.random.fold_in(own_key, 6)
    for dim, parts in pieces:
        draws = jnp.exp(jax.random.uniform(jax.random.fold_in(own, dim), (parts,), jnp.float32, low / len(pieces), high / len(pieces)))
        gain = gain * jnp.repeat(draws, dims[dim] // parts).reshape([-1 if axis == dim else 1 for axis in range(len(dims))])
    return gain


def gaussian(stream_key, shape, scale, bound, cuts=(), held_as=jnp.bfloat16):
    gain = level_of(stream_key, shape, cuts, -0.22, 0.18) if cuts else 1.0
    drawn = jax.random.normal(stream_key, shape, jnp.float32) * scale * gain
    return jnp.minimum(jnp.maximum(drawn, -bound), bound).astype(held_as)


def setup_inputs(seed: int = 0) -> dict:
    arg_keys = jax.random.split(jax.random.key(seed), 6)
    feats_t = gaussian(arg_keys[0], (F_IN, NODES), 1.0, 6.0, ((0, 4), (1, 8)))
    adj_index = draw_adj_index(jax.random.fold_in(arg_keys[5], 71), 0)
    adj_weight = draw_adj_weight(jax.random.fold_in(arg_keys[5], 71), 0)
    weight = gaussian(arg_keys[3], (F_IN, UNITS), F_IN ** -0.5, 0.5)
    cotangent_t = gaussian(arg_keys[4], (UNITS, NODES), 1.0, 6.0, ((0, 4), (1, 8)))
    return {"feats_t": feats_t, "adj_index": adj_index, "adj_weight": adj_weight, "weight": weight, "cotangent_t": cotangent_t}


def reference(feats_t, adj_index, adj_weight, weight, cotangent_t):
    feat_blocks = feats_t.reshape(F_IN, NB, TILE)

    def aggregate(block_id):
        picked = jnp.take(feat_blocks, adj_index[block_id], axis=1).astype(jnp.float32)
        return jnp.einsum('fkj,kij->fi', picked, adj_weight[block_id].astype(jnp.float32), precision=lax.Precision.HIGHEST)
    summed = lax.map(aggregate, jnp.arange(NB))
    aggregated = summed.transpose(1, 0, 2).reshape(F_IN, NODES).astype(jnp.bfloat16)
    pre_act = jnp.dot(weight.T, aggregated, preferred_element_type=jnp.float32)
    output_t = jax.nn.silu(pre_act).astype(jnp.bfloat16)
    sigm = jax.nn.sigmoid(pre_act)
    pre_grad = (cotangent_t.astype(jnp.float32) * sigm * (1.0 + pre_act * (1.0 - sigm))).astype(jnp.bfloat16)
    weight_grad = jnp.dot(aggregated, pre_grad.T, preferred_element_type=jnp.float32) / jnp.sqrt(jnp.float32(NODES))
    agg_grad = jnp.dot(weight, pre_grad, preferred_element_type=jnp.float32).astype(jnp.bfloat16)
    grad_blocks = agg_grad.reshape(F_IN, NB, TILE)

    def spread(accum, block_id):
        terms = jnp.einsum('fi,kij->kfj', grad_blocks[:, block_id].astype(jnp.float32), adj_weight[block_id].astype(jnp.float32), precision=lax.Precision.HIGHEST)
        return (accum.at[adj_index[block_id]].add(terms), None)
    accum, _ = lax.scan(spread, jnp.zeros((NB, F_IN, TILE), jnp.float32), jnp.arange(NB))
    feat_grad = accum.transpose(1, 0, 2).reshape(F_IN, NODES)
    return (output_t, weight_grad, feat_grad)
```

```python
import functools
import math

import jax
import jax.numpy as jnp
from jax import lax
from jax.experimental import pallas as pl
from jax.experimental.pallas import tpu as pltpu
from jax.sharding import PartitionSpec as P

CAP = 4
LANES = 128
SEL = 16
IDS = 24
TAB = 32
F32, BF16, I32 = jnp.float32, jnp.bfloat16, jnp.int32
VMEM = pltpu.MemorySpace.VMEM


def masks_of(rows_n):
    half = rows_n // 2
    even = list(range(1, half)) + [0]
    odd = [rows_n - 2 - k for k in range(half - 1)] + [rows_n - 1]
    return even, odd


def whole(shape):
    zeros = (0,) * len(shape)
    return pl.BlockSpec(shape, lambda *_: zeros)


def call(kernel, grid, in_specs, out_specs, out_shape, scratch, prefetch, flops, nbytes, vmem, name):
    return pl.pallas_call(
        kernel,
        out_shape=out_shape,
        grid_spec=pltpu.PrefetchScalarGridSpec(
            num_scalar_prefetch=prefetch,
            grid=grid,
            in_specs=in_specs,
            out_specs=out_specs,
            scratch_shapes=scratch,
        ),
        compiler_params=pltpu.CompilerParams(
            dimension_semantics=("arbitrary",) * len(grid), vmem_limit_bytes=vmem
        ),
        cost_estimate=pl.CostEstimate(flops=flops, bytes_accessed=nbytes, transcendentals=0),
        name=name,
    )


def iota(shape, dim):
    return lax.broadcasted_iota(I32, shape, dim)


def index_kernel(rows_n, blk, adj_ref, out_ref):
    slots_n, ids_n = adj_ref.shape
    r = lax.axis_index("rows")
    col = lax.axis_index("cols")
    c = lax.rem(col, 2)
    half = rows_n // 2
    adj = adj_ref[...]
    mine = r * blk + iota((blk, ids_n), 0)
    hits = jnp.zeros((blk, ids_n), F32)
    for k in range(slots_n):
        hits += (adj[k : k + 1, :] == mine).astype(F32)
    group = (iota((ids_n, LANES), 0) // blk == iota((ids_n, LANES), 1)).astype(BF16)
    wants = jnp.dot(hits.astype(BF16), group, preferred_element_type=F32) > 0.5
    below = (iota((blk, blk), 1) < iota((blk, blk), 0)).astype(BF16)
    order = jnp.dot(below, wants.astype(BF16), preferred_element_type=F32)
    number = iota((blk, LANES), 0).astype(F32)
    for o in range(CAP):
        pick = jnp.where(wants & (jnp.abs(order - o) < 0.5), number, 0.0)
        out_ref[SEL + o : SEL + o + 1, :] = jnp.sum(pick, axis=0, keepdims=True).astype(I32)
    start = pl.multiple_of((r * blk) // LANES * LANES, LANES)
    near = adj_ref[:, pl.ds(start, LANES)]
    block = iota((ids_n, LANES), 0)
    seen = jnp.zeros((ids_n, LANES), F32)
    for k in range(slots_n):
        seen += (near[k : k + 1, :] == block).astype(F32)
    own = ((iota((LANES, LANES), 0) + start) // blk == r).astype(BF16)
    needed = jnp.dot(seen.astype(BF16), own, preferred_element_type=F32) > 0.5
    a, b = iota((ids_n, ids_n), 0), iota((ids_n, ids_n), 1)
    earlier = ((b < a) & (a // blk == b // blk)).astype(BF16)
    place = jnp.dot(earlier, needed.astype(BF16), preferred_element_type=F32).astype(I32)
    m = (block // blk) ^ r
    step = jnp.where(m < half, m - 1, jnp.where(m == rows_n - 1, half - 1, rows_n - 2 - m))
    other = jnp.where((m < half) == (c == 0), 0, half * CAP)
    slot = jnp.where(m == 0, block % blk, blk + other + step * CAP + place).astype(F32)
    for k in range(slots_n):
        found = jnp.where(near[k : k + 1, :] == block, slot, 0.0)
        out_ref[k : k + 1, :] = jnp.sum(found, axis=0, keepdims=True).astype(I32)
    lane = iota((1, LANES), 1)
    x = col // 2
    lane0 = r * blk - start
    eighth = lane0
    ids = jnp.where(lane == 0, r, jnp.where(lane == 1, c, jnp.where(lane == 2, x, eighth)))
    out_ref[IDS : IDS + 1, :] = ids.astype(I32)


def mask_at(masks, k, c):
    return jnp.where(c == 0, masks[0][k], masks[1][k])


def pack_kernel(masks, blk, tile, tab, mine, mate, cot, own, *outs):
    sends, cots = outs[: len(masks[0])], outs[len(masks[0]) :]
    r, c, x = tab[IDS, 0], tab[IDS, 1], tab[IDS, 2]
    f = mine.shape[0]
    top = pl.multiple_of(c * f, f)
    low = pl.multiple_of((1 - c) * f, f)
    for k in range(len(masks[0])):
        d = r ^ mask_at(masks, k, c)
        for o in range(CAP):
            at = pl.multiple_of(tab[SEL + o, d] * tile, tile)
            sends[k][o, pl.ds(top, f), :] = mine[:, pl.ds(at, tile)]
            sends[k][o, pl.ds(low, f), :] = mate[:, pl.ds(at, tile)]
    for b in range(blk):
        own[b, pl.ds(top, f), :] = mine[:, b * tile : (b + 1) * tile]
        own[b, pl.ds(low, f), :] = mate[:, b * tile : (b + 1) * tile]
    width = cots[0].shape[1]
    for q in range(4):
        at = pl.multiple_of(((c ^ (q & 1)) * 2 + (x ^ (q >> 1))) * width, width)
        cots[q][...] = cot[:, pl.ds(at, width)]


def gather_kernel(first_of, steps, blk, tab, a_ref, own, *rest):
    recvs, out, table = rest[: 2 * steps], rest[2 * steps], rest[2 * steps + 1]
    t = pl.program_id(0)

    @pl.when(t == 0)
    def _():
        table[:blk] = own[...]
        for k in range(2 * steps):
            table[blk + k * CAP : blk + (k + 1) * CAP] = recvs[k][...]

    lane = tab[IDS, 3] + first_of(tab) + t
    slots_n = a_ref.shape[1]
    acc = None
    for k in range(0, slots_n, 2):
        left = jnp.concatenate([table[tab[k, lane]], table[tab[k + 1, lane]]], axis=1)
        right = jnp.concatenate([a_ref[0, k], a_ref[0, k + 1]], axis=1)
        part = lax.dot_general(left, right, (((1,), (1,)), ((), ())), preferred_element_type=F32)
        acc = part if acc is None else acc + part
    out[...] = acc.astype(BF16)


def dense_kernel(tab, keep, came, w_ref, c0, c1, c2, c3, *rest):
    outs, (g_send, g_keep), wgs = rest[:4], rest[4:6], rest[6:10]
    agg, cot, pre_s, out_s, grad_s, wg_s = rest[10:]
    c, x = tab[IDS, 1], tab[IDS, 2]
    fx = keep.shape[0]
    u = c0.shape[0]
    col = 2 * x + c
    agg[pl.ds(pl.multiple_of(x * fx, fx), fx), :] = keep[...]
    agg[pl.ds(pl.multiple_of((1 - x) * fx, fx), fx), :] = came[...]
    for q, piece in enumerate((c0, c1, c2, c3)):
        cot[pl.ds(pl.multiple_of((col ^ q) * u, u), u), :] = piece[...]
    w = w_ref[...]
    act = agg[...]
    pre_act = lax.dot_general(w, act, (((0,), (0,)), ((), ())), preferred_element_type=F32)
    sigm = jax.nn.sigmoid(pre_act)
    out_s[...] = (pre_act * sigm).astype(BF16)
    pre = (cot[...].astype(F32) * sigm * (1.0 + pre_act * (1.0 - sigm))).astype(BF16)
    pre_s[...] = pre
    grad_s[...] = jnp.dot(w, pre, preferred_element_type=F32).astype(BF16)
    wg_s[...] = lax.dot_general(act, pre, (((1,), (1,)), ((), ())), preferred_element_type=F32)
    g_keep[...] = grad_s[pl.ds(pl.multiple_of(x * fx, fx), fx), :]
    g_send[...] = grad_s[pl.ds(pl.multiple_of((1 - x) * fx, fx), fx), :]
    f = wgs[0].shape[0]
    for q in range(4):
        outs[q][...] = out_s[pl.ds(pl.multiple_of((col ^ q) * u, u), u), :]
        wgs[q][...] = wg_s[pl.ds(pl.multiple_of((col ^ q) * f, f), f), :]


def spread_step(first_of, tab, a_ref, g_ref, acc):
    t = pl.program_id(0)
    lane = tab[IDS, 3] + first_of(tab) + t
    tile = g_ref.shape[1]
    g = g_ref[...]
    for k in range(0, a_ref.shape[1], 2):
        right = jnp.concatenate([a_ref[0, k], a_ref[0, k + 1]], axis=1)
        part = jnp.dot(g, right, preferred_element_type=F32)
        acc[tab[k, lane]] += part[:, :tile]
        acc[tab[k + 1, lane]] += part[:, tile:]


def spread_first_kernel(first_of, tab, a_ref, g_ref, acc):
    @pl.when(pl.program_id(0) == 0)
    def _():
        acc[...] = jnp.zeros_like(acc)

    spread_step(first_of, tab, a_ref, g_ref, acc)


def spread_last_kernel(first_of, steps, blk, tab, a_ref, g_ref, before, own, stay, *rest):
    sends, acc = rest[:steps], rest[steps]

    @pl.when(pl.program_id(0) == 0)
    def _():
        acc[...] = before[...]

    spread_step(first_of, tab, a_ref, g_ref, acc)

    @pl.when(pl.program_id(0) == pl.num_programs(0) - 1)
    def _():
        tile = g_ref.shape[1]
        for b in range(blk):
            own[:, b * tile : (b + 1) * tile] = acc[b]
        stay[...] = acc[blk : blk + steps * CAP]
        for k in range(steps):
            at = blk + (steps + k) * CAP
            sends[k][...] = acc[at : at + CAP].astype(BF16)


def collect_kernel(masks, tab, own, *rest):
    steps = len(masks[0])
    recvs, keep, send, acc = rest[:steps], rest[steps], rest[steps + 1], rest[steps + 2]
    r, c = tab[IDS, 0], tab[IDS, 1]
    tile = recvs[0].shape[2]
    f = keep.shape[0]
    acc[...] = own[...]

    def add(k):
        d = r ^ mask_at(masks, k, c)
        for o in range(CAP):
            at = pl.ds(pl.multiple_of(tab[SEL + o, d] * tile, tile), tile)
            acc[:, at] += recvs[k][o].astype(F32)

    for k in range(steps - 1):
        add(k)

    @pl.when(c == 1)
    def _():
        add(steps - 1)

    keep[...] = acc[pl.ds(pl.multiple_of(c * f, f), f), :]
    send[...] = acc[pl.ds(pl.multiple_of((1 - c) * f, f), f), :]


def place_kernel(tab, p0, p1, p2, p3, out):
    c, x = tab[IDS, 1], tab[IDS, 2]
    width = p0.shape[1]
    for q, piece in enumerate((p0, p1, p2, p3)):
        at = pl.multiple_of(((c ^ (q & 1)) * 2 + (x ^ (q >> 1))) * width, width)
        out[:, pl.ds(at, width)] = piece[...]


def body(feats_t, adj_index, adj_weight, weight, cotangent_t):
    f, nodes = feats_t.shape
    blk, slots_n, tile, _ = adj_weight.shape
    units_loc = cotangent_t.shape[0]
    f_in, units = weight.shape
    rows_n, cols_n = lax.axis_size("rows"), lax.axis_size("cols")
    assert cols_n == 4 and rows_n & (rows_n - 1) == 0 and blk % 4 == 0
    masks = masks_of(rows_n)
    steps = len(masks[0])
    table_n = blk + 2 * steps * CAP
    fx = 2 * f
    quarter = nodes // 4
    per = blk // 4
    mib = 1 << 20
    sds = jax.ShapeDtypeStruct

    def mate(v, q):
        return lax.ppermute(v, "cols", [(i, i ^ q) for i in range(cols_n)])

    def over_rows(v, k):
        pairs = []
        for i in range(rows_n):
            for j in range(cols_n):
                m = masks[j % 2][k]
                if m:
                    pairs.append((i * cols_n + j, (i ^ m) * cols_n + j))
        return lax.ppermute(v, ("rows", "cols"), pairs)

    feats_mate = mate(feats_t, 1)
    tab = pl.pallas_call(
        functools.partial(index_kernel, rows_n, blk),
        out_shape=sds((TAB, LANES), I32),
        cost_estimate=pl.CostEstimate(flops=10**7, bytes_accessed=10**5, transcendentals=0),
        name="index",
    )(adj_index.T)

    part = sds((CAP, fx, tile), BF16)
    piece = sds((units_loc, quarter), BF16)
    own_t, *rest = call(
        functools.partial(pack_kernel, masks, blk, tile), (1,),
        [whole((f, nodes)), whole((f, nodes)), whole((units_loc, nodes))],
        [whole((blk, fx, tile))] + [whole(part.shape)] * steps + [whole(piece.shape)] * 4,
        [sds((blk, fx, tile), BF16)] + [part] * steps + [piece] * 4,
        [], 1, 10**6, 2 * mib, 16 * mib, "pack",
    )(tab, feats_t, feats_mate, cotangent_t)
    sends, cots = rest[:steps], rest[steps:]
    got = [over_rows(s, k) for k, s in enumerate(sends)]
    cots = [cots[0]] + [mate(cots[q], q) for q in (1, 2, 3)]
    got_mate = [mate(g, 1) for g in got]

    def far_first(t):
        return t[IDS, 1] * (2 * per) + (1 - t[IDS, 2]) * per

    def near_first(t):
        return t[IDS, 1] * (2 * per) + t[IDS, 2] * per

    def a_spec(first_of):
        return pl.BlockSpec(
            (1, slots_n, tile, tile), lambda t, tab: (first_of(tab) + t, 0, 0, 0)
        )

    a_flops = 2 * per * slots_n * fx * tile * tile
    a_bytes = 2 * per * slots_n * tile * tile

    def gather(first_of, name):
        return call(
            functools.partial(gather_kernel, first_of, steps, blk), (per,),
            [a_spec(first_of), whole((blk, fx, tile))] + [whole(part.shape)] * (2 * steps),
            pl.BlockSpec((fx, tile), lambda t, tab: (0, t)),
            sds((fx, quarter), BF16),
            [pltpu.VMEM((table_n, fx, tile), BF16)],
            1, a_flops, a_bytes, 32 * mib, name,
        )(tab, adj_weight, own_t, *got, *got_mate)

    agg_far = gather(far_first, "gather_far")
    agg_came = mate(agg_far, 2)
    agg_near = gather(near_first, "gather_near")

    half_g = sds((fx, quarter), BF16)
    wg_part = sds((f, units), F32)
    *outs, g_send, g_keep, w0, w1, w2, w3 = call(
        dense_kernel, (1,),
        [whole((fx, quarter))] * 2 + [whole((f_in, units))] + [whole(piece.shape)] * 4,
        [whole(piece.shape)] * 4 + [whole(half_g.shape)] * 2 + [whole(wg_part.shape)] * 4,
        [piece] * 4 + [half_g] * 2 + [wg_part] * 4,
        [
            pltpu.VMEM((f_in, quarter), BF16),
            pltpu.VMEM((units, quarter), BF16),
            pltpu.VMEM((units, quarter), BF16),
            pltpu.VMEM((units, quarter), BF16),
            pltpu.VMEM((f_in, quarter), BF16),
            pltpu.VMEM((f_in, units), F32),
        ],
        1, 6 * f_in * units * quarter, 2 * mib, 32 * mib, "dense",
    )(tab, agg_near, agg_came, weight, *cots)
    g_came = mate(g_send, 2)
    wg = w0 + mate(w1, 1) + mate(w2, 2) + mate(w3, 3)
    step = 1
    while step < rows_n:
        pairs = [(i, i ^ step) for i in range(rows_n)]
        wg = wg + lax.ppermute(wg, "rows", pairs)
        step *= 2
    weight_grad = wg * (1.0 / math.sqrt(nodes * rows_n))

    acc_t = sds((table_n, fx, tile), F32)
    g_spec = pl.BlockSpec((fx, tile), lambda t, tab: (0, t))
    acc = call(
        functools.partial(spread_first_kernel, near_first), (per,),
        [a_spec(near_first), g_spec], whole(acc_t.shape), acc_t,
        [], 1, a_flops, a_bytes, 32 * mib, "spread_near",
    )(tab, adj_weight, g_keep)
    own_acc, stay, *grads = call(
        functools.partial(spread_last_kernel, far_first, steps, blk), (per,),
        [a_spec(far_first), g_spec, whole(acc_t.shape)],
        [whole((fx, nodes)), whole((steps * CAP, fx, tile))] + [whole(part.shape)] * steps,
        [sds((fx, nodes), F32), sds((steps * CAP, fx, tile), F32)] + [part] * steps,
        [pltpu.VMEM(acc_t.shape, F32)],
        1, a_flops, a_bytes, 48 * mib, "spread_far",
    )(tab, adj_weight, g_came, acc)
    back = []
    for k in range(steps):
        total = stay[k * CAP : (k + 1) * CAP] + mate(grads[k], 1).astype(F32)
        back.append(over_rows(total.astype(BF16), k))
    keep, send = call(
        functools.partial(collect_kernel, masks), (1,),
        [whole((fx, nodes))] + [whole(part.shape)] * steps,
        [whole((f, nodes))] * 2,
        [sds((f, nodes), F32)] * 2,
        [pltpu.VMEM((fx, nodes), F32)],
        1, 10**6, 2 * mib, 16 * mib, "collect",
    )(tab, own_acc, *back)
    feat_grad = keep + mate(send, 1)

    outs = [outs[0]] + [mate(outs[q], q) for q in (1, 2, 3)]
    output_t = call(
        place_kernel, (1,),
        [whole(piece.shape)] * 4, whole((units_loc, nodes)), sds((units_loc, nodes), BF16),
        [], 1, 10**5, mib // 2, 8 * mib, "place",
    )(tab, *outs)
    return output_t, weight_grad, feat_grad


def solution(mesh):
    return jax.shard_map(
        body,
        mesh=mesh,
        in_specs=(P("cols", "rows"), P(), P("rows", None, None, None), P(), P("cols", "rows")),
        out_specs=(P("cols", "rows"), P("cols", None), P("cols", "rows")),
        check_vma=False,
    )
```

```python
import functools
import math

import jax
import jax.numpy as jnp
from jax import lax
from jax.experimental import pallas as pl
from jax.experimental.pallas import tpu as pltpu
from jax.sharding import PartitionSpec as P

CAP = 4
LANES = 128
F32, BF16, I32 = jnp.float32, jnp.bfloat16, jnp.int32
VMEM = pl.BlockSpec(memory_space=pltpu.VMEM)
SMEM = pl.BlockSpec(memory_space=pltpu.SMEM)
HBM = pl.BlockSpec(memory_space=pltpu.HBM)
MIB = 1 << 20


def masks_of(rows_n):
    return list(range(rows_n - 1, 0, -2)), list(range(rows_n - 2, -1, -2))


def call(kernel, in_specs, out_shape, args, scratch=(), flops=10**6, mib=8):
    outs = out_shape if isinstance(out_shape, list) else [out_shape]
    nbytes = sum(a.size * a.dtype.itemsize for a in args)
    return pl.pallas_call(
        kernel,
        out_shape=[pltpu.VMEM(s, d) for s, d in outs]
        if isinstance(out_shape, list)
        else pltpu.VMEM(*out_shape),
        in_specs=in_specs,
        out_specs=[VMEM] * len(outs) if isinstance(out_shape, list) else VMEM,
        scratch_shapes=list(scratch),
        compiler_params=pltpu.CompilerParams(vmem_limit_bytes=mib * MIB),
        cost_estimate=pl.CostEstimate(flops=flops, bytes_accessed=nbytes, transcendentals=0),
    )(*args)


def iota(shape, dim):
    return lax.broadcasted_iota(I32, shape, dim)


def position():
    col = lax.axis_index("cols")
    return lax.axis_index("rows"), lax.rem(col, 2), col // 2


def rows_at(start, size):
    return pl.ds(pl.multiple_of(start * size, size), size)


def choose_kernel(blk, adj_ref, feats, sel, copied, sem):
    copy = pltpu.make_async_copy(feats, copied, sem)
    copy.start()
    slots_n, ids_n = adj_ref.shape
    r, _, _ = position()
    adj = adj_ref[...]
    mine = r * blk + iota((blk, ids_n), 0)
    hits = jnp.zeros((blk, ids_n), F32)
    for k in range(slots_n):
        hits += (adj[k : k + 1, :] == mine).astype(F32)
    group = (iota((ids_n, LANES), 0) // blk == iota((ids_n, LANES), 1)).astype(BF16)
    wants = jnp.dot(hits.astype(BF16), group, preferred_element_type=F32) > 0.5
    below = (iota((blk, blk), 1) < iota((blk, blk), 0)).astype(BF16)
    order = jnp.dot(below, wants.astype(BF16), preferred_element_type=F32)
    number = iota((blk, LANES), 0).astype(F32)
    for o in range(CAP):
        pick = jnp.where(wants & (jnp.abs(order - o) < 0.5), number, 0.0)
        sel[o : o + 1, :] = jnp.sum(pick, axis=0, keepdims=True).astype(I32)
    copy.wait()


def slot_kernel(rows_n, blk, adj_ref, out_ref):
    slots_n, ids_n = adj_ref.shape
    r, c, _ = position()
    start = pl.multiple_of((r * blk) // LANES * LANES, LANES)
    near = adj_ref[:, pl.ds(start, LANES)]
    block = iota((ids_n, LANES), 0)
    seen = jnp.zeros((ids_n, LANES), F32)
    for k in range(slots_n):
        seen += (near[k : k + 1, :] == block).astype(F32)
    own = ((iota((LANES, LANES), 0) + start) // blk == r).astype(BF16)
    needed = jnp.dot(seen.astype(BF16), own, preferred_element_type=F32) > 0.5
    a, b = iota((ids_n, ids_n), 0), iota((ids_n, ids_n), 1)
    earlier = ((b < a) & (a // blk == b // blk)).astype(BF16)
    place = jnp.dot(earlier, needed.astype(BF16), preferred_element_type=F32).astype(I32)
    m = (block // blk) ^ r
    step = (rows_n - 1 - m) // 2
    other = jnp.where((m & 1) + c == 1, 0, rows_n // 2 * CAP)
    slot = jnp.where(m == 0, block % blk, blk + other + step * CAP + place).astype(F32)
    for k in range(slots_n):
        found = jnp.where(near[k : k + 1, :] == block, slot, 0.0)
        out_ref[k : k + 1, :] = jnp.sum(found, axis=0, keepdims=True).astype(I32)


def mask_at(masks, k, c):
    return jnp.where(c == 0, masks[0][k], masks[1][k])


def pack_kernel(masks, blk, sel, mine, mate, own, *sends):
    r, c, _ = position()
    f = mine.shape[0]
    tile = own.shape[2]
    top, low = rows_at(c, f), rows_at(1 - c, f)
    for k in range(len(masks[0])):
        d = r ^ mask_at(masks, k, c)
        for o in range(CAP):
            at = rows_at(sel[o, d], tile)
            sends[k][o, top, :] = mine[:, at]
            sends[k][o, low, :] = mate[:, at]
    for b in range(blk):
        own[b, top, :] = mine[:, b * tile : (b + 1) * tile]
        own[b, low, :] = mate[:, b * tile : (b + 1) * tile]


def fetch_kernel(a_hbm, cot, a_half, c0, c1, c2, c3, sems):
    _, c, x = position()
    n = a_half.shape[0]
    width = c0.shape[1]
    copies = []
    for q, piece in enumerate((c1, c2, c3, c0)):
        q = (q + 1) % 4
        at = rows_at((c ^ (q & 1)) * 2 + (x ^ (q >> 1)), width)
        copies.append(pltpu.make_async_copy(cot.at[:, at], piece, sems.at[q]))
    for i in range(n):
        copies.append(pltpu.make_async_copy(a_hbm.at[c * n + i], a_half.at[i], sems.at[4 + i]))
    for copy in copies:
        copy.start()
    for copy in copies:
        copy.wait()


def gather_kernel(side_of, blk, slot, a_half, own, *rest):
    recvs, out, table = rest[:-2], rest[-2], rest[-1]
    r, c, x = position()
    table[:blk] = own[...]
    for k, recv in enumerate(recvs):
        table[blk + k * CAP : blk + (k + 1) * CAP] = recv[...]
    n, slots_n, tile, _ = a_half.shape
    first = side_of(x) * (n // 2)
    lane = lax.rem(r * 2 * n, LANES) + c * n + first
    for t in range(n // 2):
        acc = None
        for k in range(0, slots_n, 2):
            left = [table[slot[k + h, lane + t]] for h in range(2)]
            right = [a_half[first + t, k + h] for h in range(2)]
            part = lax.dot_general(
                jnp.concatenate(left, axis=1),
                jnp.concatenate(right, axis=1),
                (((1,), (1,)), ((), ())),
                preferred_element_type=F32,
            )
            acc = part if acc is None else acc + part
        out[:, t * tile : (t + 1) * tile] = acc.astype(BF16)


def dense_kernel(keep, came, w_ref, c0, c1, c2, c3, *rest):
    outs, (g_send, g_keep), wgs = rest[:4], rest[4:6], rest[6:10]
    agg, cot, out_s, grad_s, wg_s = rest[10:]
    _, c, x = position()
    fx = keep.shape[0]
    u = c0.shape[0]
    col = 2 * x + c
    agg[rows_at(x, fx), :] = keep[...]
    agg[rows_at(1 - x, fx), :] = came[...]
    for q, piece in enumerate((c0, c1, c2, c3)):
        cot[rows_at(col ^ q, u), :] = piece[...]
    w = w_ref[...]
    act = agg[...]
    pre_act = lax.dot_general(w, act, (((0,), (0,)), ((), ())), preferred_element_type=F32)
    sigm = jax.nn.sigmoid(pre_act)
    out_s[...] = (pre_act * sigm).astype(BF16)
    pre = (cot[...].astype(F32) * sigm * (1.0 + pre_act * (1.0 - sigm))).astype(BF16)
    grad_s[...] = jnp.dot(w, pre, preferred_element_type=F32).astype(BF16)
    wg_s[...] = lax.dot_general(act, pre, (((1,), (1,)), ((), ())), preferred_element_type=F32)
    g_keep[...] = grad_s[rows_at(x, fx), :]
    g_send[...] = grad_s[rows_at(1 - x, fx), :]
    f = wgs[0].shape[0]
    for q in range(4):
        outs[q][...] = out_s[rows_at(col ^ q, u), :]
        wgs[q][...] = wg_s[rows_at(col ^ q, f), :]


def spread(side_of, slot, a_half, g_ref, acc):
    r, c, x = position()
    n, slots_n, tile, _ = a_half.shape
    first = side_of(x) * (n // 2)
    lane = lax.rem(r * 2 * n, LANES) + c * n + first
    for t in range(n // 2):
        g = g_ref[:, t * tile : (t + 1) * tile]
        for k in range(0, slots_n, 2):
            right = jnp.concatenate([a_half[first + t, k], a_half[first + t, k + 1]], axis=1)
            part = jnp.dot(g, right, preferred_element_type=F32)
            acc[slot[k, lane + t]] += part[:, :tile]
            acc[slot[k + 1, lane + t]] += part[:, tile:]


def spread_first_kernel(side_of, slot, a_half, g_ref, acc):
    acc[...] = jnp.zeros_like(acc)
    spread(side_of, slot, a_half, g_ref, acc)


def spread_last_kernel(side_of, steps, blk, slot, a_half, g_ref, before, own, stay, *rest):
    sends, acc = rest[:steps], rest[steps]
    acc[...] = before[...]
    spread(side_of, slot, a_half, g_ref, acc)
    tile = g_ref.shape[1] // (a_half.shape[0] // 2)
    for k in range(steps):
        at = blk + (steps + k) * CAP
        sends[k][...] = acc[at : at + CAP].astype(BF16)
    for b in range(blk):
        own[:, b * tile : (b + 1) * tile] = acc[b]
    stay[...] = acc[blk : blk + steps * CAP]


def collect_kernel(masks, sel, own, *rest):
    steps = len(masks[0])
    recvs, keep, send, acc = rest[:steps], rest[steps], rest[steps + 1], rest[steps + 2]
    r, c, _ = position()
    tile = recvs[0].shape[2]
    f = keep.shape[0]
    acc[...] = own[...]

    def add(k):
        d = r ^ mask_at(masks, k, c)
        for o in range(CAP):
            acc[:, rows_at(sel[o, d], tile)] += recvs[k][o].astype(F32)

    for k in range(steps - 1):
        add(k)

    @pl.when(c == 0)
    def _():
        add(steps - 1)

    keep[...] = acc[rows_at(c, f), :]
    send[...] = acc[rows_at(1 - c, f), :]


def place_kernel(p0, p1, p2, p3, out):
    _, c, x = position()
    width = p0.shape[1]
    for q, piece in enumerate((p0, p1, p2, p3)):
        out[:, rows_at((c ^ (q & 1)) * 2 + (x ^ (q >> 1)), width)] = piece[...]


def layer(feats_t, adj_index, adj_weight, weight, cotangent_t):
    f, nodes = feats_t.shape
    blk, slots_n, tile, _ = adj_weight.shape
    units_loc = cotangent_t.shape[0]
    f_in, units = weight.shape
    rows_n, cols_n = lax.axis_size("rows"), lax.axis_size("cols")
    assert cols_n == 4 and rows_n & (rows_n - 1) == 0 and blk % 4 == 0
    masks = masks_of(rows_n)
    steps = len(masks[0])
    table_n = blk + 2 * steps * CAP
    fx = 2 * f
    quarter = nodes // 4
    half = blk // 2
    big = min(48, 8 + rows_n)

    def mate(v, q):
        return lax.ppermute(v, "cols", [(i, i ^ q) for i in range(cols_n)])

    def over_rows(v, k):
        pairs = []
        for i in range(rows_n):
            for j in range(cols_n):
                m = masks[j % 2][k]
                if m:
                    pairs.append((i * cols_n + j, (i ^ m) * cols_n + j))
        return lax.ppermute(v, ("rows", "cols"), pairs)

    adj_t = adj_index.T
    in_hbm = functools.partial(pltpu.with_memory_space_constraint, memory_space=pltpu.HBM)
    feats_mate = mate(feats_t, 1)
    sel, feats = call(
        functools.partial(choose_kernel, blk), [VMEM, HBM],
        [((8, LANES), I32), ((f, nodes), BF16)], [adj_t, in_hbm(feats_t)],
        [pltpu.SemaphoreType.DMA], mib=big,
    )
    part = ((CAP, fx, tile), BF16)
    piece = ((units_loc, quarter), BF16)
    own_t, *sends = call(
        functools.partial(pack_kernel, masks, blk), [SMEM, VMEM, VMEM],
        [((blk, fx, tile), BF16)] + [part] * steps, [sel, feats, feats_mate], mib=big,
    )
    got = [over_rows(s, k) for k, s in enumerate(sends)]
    a_half, *cots = call(
        fetch_kernel, [HBM, HBM],
        [((half, slots_n, tile, tile), BF16)] + [piece] * 4,
        [in_hbm(adj_weight), in_hbm(cotangent_t)],
        [pltpu.SemaphoreType.DMA((4 + half,))],
    )
    slot = call(
        functools.partial(slot_kernel, rows_n, blk), [VMEM],
        ((slots_n, LANES), I32), [adj_t], mib=big,
    )
    cots = [cots[0]] + [mate(cots[q], q) for q in (1, 2, 3)]
    got_mate = [mate(g, 1) for g in got]

    def far(x):
        return 1 - x

    def near(x):
        return x

    a_flops = half * slots_n * fx * tile * tile

    def gather(side_of):
        args = [slot, a_half, own_t, *got, *got_mate]
        return call(
            functools.partial(gather_kernel, side_of, blk), [SMEM] + [VMEM] * (len(args) - 1),
            ((fx, quarter), BF16), args, [pltpu.VMEM((table_n, fx, tile), BF16)], a_flops,
            big,
        )

    agg_far = gather(far)
    agg_came = mate(agg_far, 2)
    agg_near = gather(near)

    half_g = ((fx, quarter), BF16)
    wg_part = ((f, units), F32)
    args = [agg_near, agg_came, weight, *cots]
    *outs, g_send, g_keep, w0, w1, w2, w3 = call(
        dense_kernel, [VMEM] * len(args),
        [piece] * 4 + [half_g] * 2 + [wg_part] * 4, args,
        [
            pltpu.VMEM((f_in, quarter), BF16),
            pltpu.VMEM((units, quarter), BF16),
            pltpu.VMEM((units, quarter), BF16),
            pltpu.VMEM((f_in, quarter), BF16),
            pltpu.VMEM((f_in, units), F32),
        ],
        6 * f_in * units * quarter, 12,
    )
    g_came = mate(g_send, 2)
    wg = w0 + mate(w1, 1) + mate(w2, 2) + mate(w3, 3)
    bit = 0
    while 1 << bit < rows_n:
        wg = wg + lax.ppermute(wg, "rows", [(i, i ^ (1 << bit)) for i in range(rows_n)])
        bit += 1
    weight_grad = wg * (1.0 / math.sqrt(nodes * rows_n))

    acc = call(
        functools.partial(spread_first_kernel, near), [SMEM, VMEM, VMEM],
        ((table_n, fx, tile), F32), [slot, a_half, g_keep], [], a_flops, big,
    )
    own_acc, stay, *grads = call(
        functools.partial(spread_last_kernel, far, steps, blk),
        [SMEM, VMEM, VMEM, VMEM],
        [((fx, nodes), F32), ((steps * CAP, fx, tile), F32)] + [part] * steps,
        [slot, a_half, g_came, acc], [pltpu.VMEM((table_n, fx, tile), F32)], a_flops, big + 8,
    )
    back = []
    for k in range(steps):
        came = mate(grads[k], 1)
        total = stay[k * CAP : (k + 1) * CAP] + came.astype(F32)
        back.append(over_rows(total.astype(BF16), k))
    keep, send = call(
        functools.partial(collect_kernel, masks), [SMEM, VMEM] + [VMEM] * steps,
        [((f, nodes), F32)] * 2, [sel, own_acc, *back], [pltpu.VMEM((fx, nodes), F32)], mib=big,
    )
    feat_grad = keep + mate(send, 1)

    outs = [outs[0]] + [mate(outs[q], q) for q in (1, 2, 3)]
    output_t = pl.pallas_call(
        place_kernel,
        out_shape=jax.ShapeDtypeStruct((units_loc, nodes), BF16),
        in_specs=[VMEM] * 4,
        out_specs=VMEM,
        compiler_params=pltpu.CompilerParams(vmem_limit_bytes=4 * MIB),
        name="place",
    )(*outs)
    return output_t, weight_grad, feat_grad


def solution(mesh):
    return jax.shard_map(
        layer,
        mesh=mesh,
        in_specs=(P("cols", "rows"), P(), P("rows", None, None, None), P(), P("cols", "rows")),
        out_specs=(P("cols", "rows"), P("cols", None), P("cols", "rows")),
        check_vma=False,
    )
```

```python
import functools
import math

import jax
import jax.numpy as jnp
from jax import lax
from jax.experimental import pallas as pl
from jax.experimental.pallas import tpu as pltpu
from jax.sharding import PartitionSpec as P

CAP = 4
LANES = 128
F32, BF16, I32 = jnp.float32, jnp.bfloat16, jnp.int32
VMEM = pl.BlockSpec(memory_space=pltpu.VMEM)
SMEM = pl.BlockSpec(memory_space=pltpu.SMEM)
HBM = pl.BlockSpec(memory_space=pltpu.HBM)
MIB = 1 << 20


def call(kernel, in_specs, out_shape, args, scratch=(), flops=10**6, mib=8, out=False):
    place = jax.ShapeDtypeStruct if out else pltpu.VMEM
    outs = out_shape if isinstance(out_shape, list) else [out_shape]
    nbytes = sum(a.size * a.dtype.itemsize for a in args)
    return pl.pallas_call(
        kernel,
        out_shape=[place(s, d) for s, d in outs]
        if isinstance(out_shape, list)
        else place(*out_shape),
        in_specs=in_specs,
        out_specs=[VMEM] * len(outs) if isinstance(out_shape, list) else VMEM,
        scratch_shapes=list(scratch),
        compiler_params=pltpu.CompilerParams(vmem_limit_bytes=mib * MIB),
        cost_estimate=pl.CostEstimate(flops=flops, bytes_accessed=nbytes, transcendentals=0),
    )(*args)


def iota(shape, dim):
    return lax.broadcasted_iota(I32, shape, dim)


def position():
    col = lax.axis_index("cols")
    return lax.axis_index("rows"), lax.rem(col, 2), col // 2


def rows_at(start, size):
    return pl.ds(pl.multiple_of(start * size, size), size)


def choose_kernel(adj_ref, feats, sel, copied, sends, sel_s, sems):
    copy = pltpu.make_async_copy(feats, copied, sems.at[0])
    copy.start()
    slots_n, ids_n = adj_ref.shape
    tile = sends.shape[3]
    blk = feats.shape[1] // tile
    r, _, _ = position()
    adj = adj_ref[...]
    mine = r * blk + iota((blk, ids_n), 0)
    hits = jnp.zeros((blk, ids_n), F32)
    for k in range(slots_n):
        hits += (adj[k : k + 1, :] == mine).astype(F32)
    group = (iota((ids_n, LANES), 0) // blk == iota((ids_n, LANES), 1)).astype(BF16)
    wants = jnp.dot(hits.astype(BF16), group, preferred_element_type=F32) > 0.5
    below = (iota((blk, blk), 1) < iota((blk, blk), 0)).astype(BF16)
    order = jnp.dot(below, wants.astype(BF16), preferred_element_type=F32)
    number = iota((blk, LANES), 0).astype(F32)
    for o in range(CAP):
        pick = jnp.where(wants & (jnp.abs(order - o) < 0.5), number, 0.0)
        sel[o : o + 1, :] = jnp.sum(pick, axis=0, keepdims=True).astype(I32)
    scalars = pltpu.make_async_copy(sel, sel_s, sems.at[1])
    scalars.start()
    copy.wait()
    scalars.wait()
    for d in range(sends.shape[0]):
        for o in range(CAP):
            sends[d, o] = copied[:, rows_at(sel_s[o, d], tile)]


def slot_kernel(blk, adj_ref, out_ref):
    slots_n, ids_n = adj_ref.shape
    r, _, _ = position()
    start = pl.multiple_of((r * blk) // LANES * LANES, LANES)
    near = adj_ref[:, pl.ds(start, LANES)]
    block = iota((ids_n, LANES), 0)
    seen = jnp.zeros((ids_n, LANES), F32)
    for k in range(slots_n):
        seen += (near[k : k + 1, :] == block).astype(F32)
    own = ((iota((LANES, LANES), 0) + start) // blk == r).astype(BF16)
    needed = jnp.dot(seen.astype(BF16), own, preferred_element_type=F32) > 0.5
    a, b = iota((ids_n, ids_n), 0), iota((ids_n, ids_n), 1)
    earlier = ((b < a) & (a // blk == b // blk)).astype(BF16)
    place = jnp.dot(earlier, needed.astype(BF16), preferred_element_type=F32).astype(I32)
    source = block // blk
    slot = jnp.where(source == r, block % blk, blk + source * CAP + place).astype(F32)
    for k in range(slots_n):
        found = jnp.where(near[k : k + 1, :] == block, slot, 0.0)
        out_ref[k : k + 1, :] = jnp.sum(found, axis=0, keepdims=True).astype(I32)


def fetch_kernel(side_of, a_hbm, *rest):
    _, c, x = position()
    copies = []
    if len(rest) > 2:
        cot, a_side, *pieces, sems = rest
        width = pieces[0].shape[1]
        for q in (1, 2, 3, 0):
            at = rows_at((c ^ (q & 1)) * 2 + (x ^ (q >> 1)), width)
            copies.append(pltpu.make_async_copy(cot.at[:, at], pieces[q], sems.at[q]))
    else:
        a_side, sems = rest
    n = a_side.shape[0]
    first = (2 * c + side_of(x)) * n
    for i in range(n):
        copies.append(pltpu.make_async_copy(a_hbm.at[first + i], a_side.at[i], sems.at[4 + i]))
    for copy in copies:
        copy.start()
    for copy in copies:
        copy.wait()


def gather_kernel(side_of, slot, a_side, mine, mate, got, got_mate, out, table):
    r, c, x = position()
    f = mine.shape[0]
    top, low = rows_at(c, f), rows_at(1 - c, f)
    tile = a_side.shape[3]
    blk = mine.shape[1] // tile
    for b in range(blk):
        table[b, top, :] = mine[:, b * tile : (b + 1) * tile]
        table[b, low, :] = mate[:, b * tile : (b + 1) * tile]
    for d in range(got.shape[0]):
        for o in range(CAP):
            table[blk + d * CAP + o, top, :] = got[d, o]
            table[blk + d * CAP + o, low, :] = got_mate[d, o]
    n, slots_n, tile, _ = a_side.shape
    lane = lax.rem(r * 4 * n, LANES) + (2 * c + side_of(x)) * n
    for t in range(n):
        acc = None
        for k in range(0, slots_n, 2):
            left = [table[slot[k + h, lane + t]] for h in range(2)]
            right = [a_side[t, k + h] for h in range(2)]
            part = lax.dot_general(
                jnp.concatenate(left, axis=1),
                jnp.concatenate(right, axis=1),
                (((1,), (1,)), ((), ())),
                preferred_element_type=F32,
            )
            acc = part if acc is None else acc + part
        out[:, t * tile : (t + 1) * tile] = acc.astype(BF16)


def dense_kernel(keep, came, w_ref, c0, c1, c2, c3, *rest):
    outs, (g_send, g_keep), wgs = rest[:4], rest[4:6], rest[6:10]
    agg, cot, out_s, grad_s, wg_s = rest[10:]
    _, c, x = position()
    fx = keep.shape[0]
    u = c0.shape[0]
    col = 2 * x + c
    agg[rows_at(x, fx), :] = keep[...]
    agg[rows_at(1 - x, fx), :] = came[...]
    for q, piece in enumerate((c0, c1, c2, c3)):
        cot[rows_at(col ^ q, u), :] = piece[...]
    w = w_ref[...]
    act = agg[...]
    pre_act = lax.dot_general(w, act, (((0,), (0,)), ((), ())), preferred_element_type=F32)
    sigm = jax.nn.sigmoid(pre_act)
    out_s[...] = (pre_act * sigm).astype(BF16)
    pre = (cot[...].astype(F32) * sigm * (1.0 + pre_act * (1.0 - sigm))).astype(BF16)
    grad_s[...] = jnp.dot(w, pre, preferred_element_type=F32).astype(BF16)
    wg_s[...] = lax.dot_general(act, pre, (((1,), (1,)), ((), ())), preferred_element_type=F32)
    g_keep[...] = grad_s[rows_at(x, fx), :]
    g_send[...] = grad_s[rows_at(1 - x, fx), :]
    f = wgs[0].shape[0]
    for q in range(4):
        outs[q][...] = out_s[rows_at(col ^ q, u), :]
        wgs[q][...] = wg_s[rows_at(col ^ q, f), :]


def spread(side_of, slot, a_side, g_ref, acc):
    r, c, x = position()
    n, slots_n, tile, _ = a_side.shape
    lane = lax.rem(r * 4 * n, LANES) + (2 * c + side_of(x)) * n
    for t in range(n):
        g = g_ref[:, t * tile : (t + 1) * tile]
        for k in range(0, slots_n, 2):
            right = jnp.concatenate([a_side[t, k], a_side[t, k + 1]], axis=1)
            part = jnp.dot(g, right, preferred_element_type=F32)
            acc[slot[k, lane + t]] += part[:, :tile]
            acc[slot[k + 1, lane + t]] += part[:, tile:]


def spread_first_kernel(side_of, slot, a_side, g_ref, acc):
    acc[...] = jnp.zeros_like(acc)
    spread(side_of, slot, a_side, g_ref, acc)


def spread_last_kernel(side_of, slot, a_side, g_ref, before, own, own_send, stay, send, acc):
    acc[...] = before[...]
    spread(side_of, slot, a_side, g_ref, acc)
    _, c, _ = position()
    f = own.shape[0]
    top, low = rows_at(c, f), rows_at(1 - c, f)
    tile = a_side.shape[3]
    blk = own.shape[1] // tile
    for d in range(send.shape[0]):
        for o in range(CAP):
            stay[d, o] = acc[blk + d * CAP + o, top, :]
            send[d, o] = acc[blk + d * CAP + o, low, :].astype(BF16)
    for b in range(blk):
        own[:, b * tile : (b + 1) * tile] = acc[b, top, :]
        own_send[:, b * tile : (b + 1) * tile] = acc[b, low, :]


def collect_kernel(sel, own, came, back, out):
    tile = back.shape[3]
    out[...] = own[...] + came[...]
    for d in range(back.shape[0]):
        for o in range(CAP):
            out[:, rows_at(sel[o, d], tile)] += back[d, o].astype(F32)


def place_kernel(p0, p1, p2, p3, out):
    _, c, x = position()
    width = p0.shape[1]
    for q, piece in enumerate((p0, p1, p2, p3)):
        out[:, rows_at((c ^ (q & 1)) * 2 + (x ^ (q >> 1)), width)] = piece[...]


def layer(feats_t, adj_index, adj_weight, weight, cotangent_t):
    f, nodes = feats_t.shape
    blk, slots_n, tile, _ = adj_weight.shape
    units_loc = cotangent_t.shape[0]
    f_in, units = weight.shape
    rows_n, cols_n = lax.axis_size("rows"), lax.axis_size("cols")
    assert cols_n == 4 and rows_n & (rows_n - 1) == 0 and blk % 4 == 0
    table_n = blk + rows_n * CAP
    fx = 2 * f
    quarter = nodes // 4
    big = min(48, 8 + rows_n)

    def mate(v, q):
        return lax.ppermute(v, "cols", [(i, i ^ q) for i in range(cols_n)])

    def over_rows(v):
        return lax.all_to_all(v, "rows", 0, 0, tiled=True)

    adj_t = adj_index.T
    in_hbm = functools.partial(pltpu.with_memory_space_constraint, memory_space=pltpu.HBM)
    part = (rows_n, CAP, f, tile)
    piece = ((units_loc, quarter), BF16)
    sel, feats, sends = call(
        choose_kernel, [VMEM, HBM],
        [((8, LANES), I32), ((f, nodes), BF16), (part, BF16)], [adj_t, in_hbm(feats_t)],
        [pltpu.SMEM((8, LANES), I32), pltpu.SemaphoreType.DMA((2,))], mib=big,
    )
    feats_mate = mate(feats, 1)
    got = over_rows(sends)

    def far(x):
        return 1 - x

    def near(x):
        return x

    a_side = ((blk // 4, slots_n, tile, tile), BF16)
    sems = [pltpu.SemaphoreType.DMA((4 + blk // 4,))]
    a_far, *cots = call(
        functools.partial(fetch_kernel, far), [HBM, HBM], [a_side] + [piece] * 4,
        [in_hbm(adj_weight), in_hbm(cotangent_t)], sems,
    )
    a_near = call(
        functools.partial(fetch_kernel, near), [HBM], a_side,
        [in_hbm(adj_weight)], sems,
    )
    slot = call(
        functools.partial(slot_kernel, blk), [VMEM],
        ((slots_n, LANES), I32), [adj_t], mib=big,
    )
    cots = [cots[0]] + [mate(cots[q], q) for q in (1, 2, 3)]
    got_mate = mate(got, 1)

    a_flops = blk // 2 * slots_n * fx * tile * tile

    def gather(side_of, a_side):
        args = [slot, a_side, feats, feats_mate, got, got_mate]
        return call(
            functools.partial(gather_kernel, side_of), [SMEM] + [VMEM] * (len(args) - 1),
            ((fx, quarter), BF16), args, [pltpu.VMEM((table_n, fx, tile), BF16)], a_flops,
            big,
        )

    agg_far = gather(far, a_far)
    agg_came = mate(agg_far, 2)
    agg_near = gather(near, a_near)

    half_g = ((fx, quarter), BF16)
    wg_part = ((f, units), F32)
    args = [agg_near, agg_came, weight, *cots]
    *outs, g_send, g_keep, w0, w1, w2, w3 = call(
        dense_kernel, [VMEM] * len(args),
        [piece] * 4 + [half_g] * 2 + [wg_part] * 4, args,
        [
            pltpu.VMEM((f_in, quarter), BF16),
            pltpu.VMEM((units, quarter), BF16),
            pltpu.VMEM((units, quarter), BF16),
            pltpu.VMEM((f_in, quarter), BF16),
            pltpu.VMEM((f_in, units), F32),
        ],
        6 * f_in * units * quarter, 12,
    )
    g_came = mate(g_send, 2)
    wg = w0 + mate(w1, 1) + mate(w2, 2) + mate(w3, 3)
    bit = 0
    while 1 << bit < rows_n:
        wg = wg + lax.ppermute(wg, "rows", [(i, i ^ (1 << bit)) for i in range(rows_n)])
        bit += 1
    weight_grad = wg * (1.0 / math.sqrt(nodes * rows_n))

    acc = call(
        functools.partial(spread_first_kernel, near), [SMEM, VMEM, VMEM],
        ((table_n, fx, tile), F32), [slot, a_near, g_keep], [], a_flops, big,
    )
    own, own_send, stay, send = call(
        functools.partial(spread_last_kernel, far), [SMEM, VMEM, VMEM, VMEM],
        [((f, nodes), F32)] * 2 + [(part, F32), (part, BF16)],
        [slot, a_far, g_came, acc], [pltpu.VMEM((table_n, fx, tile), F32)], a_flops, big + 8,
    )
    total = (stay + mate(send, 1).astype(F32)).astype(BF16)
    own_came = mate(own_send, 1)
    back = over_rows(total)
    feat_grad = call(
        collect_kernel, [SMEM, VMEM, VMEM, VMEM], ((f, nodes), F32),
        [sel, own, own_came, back], mib=big, out=True,
    )

    outs = [outs[0]] + [mate(outs[q], q) for q in (1, 2, 3)]
    output_t = call(place_kernel, [VMEM] * 4, ((units_loc, nodes), BF16), outs, out=True)
    return output_t, weight_grad, feat_grad


def solution(mesh):
    return jax.shard_map(
        layer,
        mesh=mesh,
        in_specs=(P("cols", "rows"), P(), P("rows", None, None, None), P(), P("cols", "rows")),
        out_specs=(P("cols", "rows"), P("cols", None), P("cols", "rows")),
        check_vma=False,
    )
```

```python
import functools
import math

import jax
import jax.numpy as jnp
from jax import lax
from jax.experimental import pallas as pl
from jax.experimental.pallas import tpu as pltpu
from jax.sharding import PartitionSpec as P

CAP = 4
LANES = 128
F32, BF16, I32 = jnp.float32, jnp.bfloat16, jnp.int32
VMEM = pl.BlockSpec(memory_space=pltpu.VMEM)
SMEM = pl.BlockSpec(memory_space=pltpu.SMEM)
HBM = pl.BlockSpec(memory_space=pltpu.HBM)
MIB = 1 << 20


def call(kernel, in_specs, out_shape, args, scratch=(), flops=10**6, mib=8, out=False):
    place = jax.ShapeDtypeStruct if out else pltpu.VMEM
    outs = out_shape if isinstance(out_shape, list) else [out_shape]
    nbytes = sum(a.size * a.dtype.itemsize for a in args)
    return pl.pallas_call(
        kernel,
        out_shape=[place(s, d) for s, d in outs]
        if isinstance(out_shape, list)
        else place(*out_shape),
        in_specs=in_specs,
        out_specs=[VMEM] * len(outs) if isinstance(out_shape, list) else VMEM,
        scratch_shapes=list(scratch),
        compiler_params=pltpu.CompilerParams(vmem_limit_bytes=mib * MIB),
        cost_estimate=pl.CostEstimate(flops=flops, bytes_accessed=nbytes, transcendentals=0),
    )(*args)


def iota(shape, dim):
    return lax.broadcasted_iota(I32, shape, dim)


def position():
    col = lax.axis_index("cols")
    return lax.axis_index("rows"), lax.rem(col, 2), col // 2


def rows_at(start, size):
    return pl.ds(pl.multiple_of(start * size, size), size)


def choose_kernel(adj_hbm, feats, sel, copied, adj_ref, sends, sel_s, sems):
    names = pltpu.make_async_copy(adj_hbm, adj_ref, sems.at[2])
    names.start()
    copy = pltpu.make_async_copy(feats, copied, sems.at[0])
    copy.start()
    slots_n, ids_n = adj_ref.shape
    tile = sends.shape[3]
    blk = feats.shape[1] // tile
    r, _, _ = position()
    names.wait()
    adj = adj_ref[...]
    mine = r * blk + iota((blk, ids_n), 0)
    hits = jnp.zeros((blk, ids_n), F32)
    for k in range(slots_n):
        hits += (adj[k : k + 1, :] == mine).astype(F32)
    group = (iota((ids_n, LANES), 0) // blk == iota((ids_n, LANES), 1)).astype(BF16)
    wants = jnp.dot(hits.astype(BF16), group, preferred_element_type=F32) > 0.5
    below = (iota((blk, blk), 1) < iota((blk, blk), 0)).astype(BF16)
    order = jnp.dot(below, wants.astype(BF16), preferred_element_type=F32)
    number = iota((blk, LANES), 0).astype(F32)
    for o in range(CAP):
        pick = jnp.where(wants & (jnp.abs(order - o) < 0.5), number, 0.0)
        sel[o : o + 1, :] = jnp.sum(pick, axis=0, keepdims=True).astype(I32)
    scalars = pltpu.make_async_copy(sel, sel_s, sems.at[1])
    scalars.start()
    copy.wait()
    scalars.wait()
    for d in range(sends.shape[0]):
        for o in range(CAP):
            sends[d, o] = copied[:, rows_at(sel_s[o, d], tile)]


def slot_kernel(blk, adj_ref, out_ref):
    slots_n, ids_n = adj_ref.shape
    r, _, _ = position()
    start = pl.multiple_of((r * blk) // LANES * LANES, LANES)
    near = adj_ref[:, pl.ds(start, LANES)]
    block = iota((ids_n, LANES), 0)
    seen = jnp.zeros((ids_n, LANES), F32)
    for k in range(slots_n):
        seen += (near[k : k + 1, :] == block).astype(F32)
    own = ((iota((LANES, LANES), 0) + start) // blk == r).astype(BF16)
    needed = jnp.dot(seen.astype(BF16), own, preferred_element_type=F32) > 0.5
    a, b = iota((ids_n, ids_n), 0), iota((ids_n, ids_n), 1)
    earlier = ((b < a) & (a // blk == b // blk)).astype(BF16)
    place = jnp.dot(earlier, needed.astype(BF16), preferred_element_type=F32).astype(I32)
    source = block // blk
    slot = jnp.where(source == r, block % blk, blk + source * CAP + place).astype(F32)
    for k in range(slots_n):
        found = jnp.where(near[k : k + 1, :] == block, slot, 0.0)
        out_ref[k : k + 1, :] = jnp.sum(found, axis=0, keepdims=True).astype(I32)


def fetch_kernel(side_of, a_hbm, *rest):
    _, c, x = position()
    copies = []
    if len(rest) > 2:
        cot, a_side, *pieces, sems = rest
        width = pieces[0].shape[1]
        for q in (1, 2, 3, 0):
            at = rows_at((c ^ (q & 1)) * 2 + (x ^ (q >> 1)), width)
            copies.append(pltpu.make_async_copy(cot.at[:, at], pieces[q], sems.at[q]))
    else:
        a_side, sems = rest
    n = a_side.shape[0]
    first = (2 * c + side_of(x)) * n
    for i in range(n):
        copies.append(pltpu.make_async_copy(a_hbm.at[first + i], a_side.at[i], sems.at[4 + i]))
    for copy in copies:
        copy.start()
    for copy in copies:
        copy.wait()


def gather_kernel(side_of, slot, a_side, mine, mate, got, got_mate, out, table):
    r, c, x = position()
    f = mine.shape[0]
    top, low = rows_at(c, f), rows_at(1 - c, f)
    tile = a_side.shape[3]
    blk = mine.shape[1] // tile
    for b in range(blk):
        table[b, top, :] = mine[:, b * tile : (b + 1) * tile]
        table[b, low, :] = mate[:, b * tile : (b + 1) * tile]
    for d in range(got.shape[0]):
        for o in range(CAP):
            table[blk + d * CAP + o, top, :] = got[d, o]
            table[blk + d * CAP + o, low, :] = got_mate[d, o]
    n, slots_n, tile, _ = a_side.shape
    lane = lax.rem(r * 4 * n, LANES) + (2 * c + side_of(x)) * n
    for t in range(n):
        acc = None
        for k in range(0, slots_n, 2):
            left = [table[slot[k + h, lane + t]] for h in range(2)]
            right = [a_side[t, k + h] for h in range(2)]
            part = lax.dot_general(
                jnp.concatenate(left, axis=1),
                jnp.concatenate(right, axis=1),
                (((1,), (1,)), ((), ())),
                preferred_element_type=F32,
            )
            acc = part if acc is None else acc + part
        out[:, t * tile : (t + 1) * tile] = acc.astype(BF16)


def dense_kernel(keep, came, w_ref, c0, c1, c2, c3, *rest):
    outs, (g_send, g_keep), wgs = rest[:4], rest[4:6], rest[6:10]
    agg, cot, out_s, grad_s, wg_s = rest[10:]
    _, c, x = position()
    fx = keep.shape[0]
    u = c0.shape[0]
    col = 2 * x + c
    agg[rows_at(x, fx), :] = keep[...]
    agg[rows_at(1 - x, fx), :] = came[...]
    for q, piece in enumerate((c0, c1, c2, c3)):
        cot[rows_at(col ^ q, u), :] = piece[...]
    w = w_ref[...]
    act = agg[...]
    pre_act = lax.dot_general(w, act, (((0,), (0,)), ((), ())), preferred_element_type=F32)
    sigm = jax.nn.sigmoid(pre_act)
    out_s[...] = (pre_act * sigm).astype(BF16)
    pre = (cot[...].astype(F32) * sigm * (1.0 + pre_act * (1.0 - sigm))).astype(BF16)
    grad_s[...] = jnp.dot(w, pre, preferred_element_type=F32).astype(BF16)
    wg_s[...] = lax.dot_general(act, pre, (((1,), (1,)), ((), ())), preferred_element_type=F32)
    g_keep[...] = grad_s[rows_at(x, fx), :]
    g_send[...] = grad_s[rows_at(1 - x, fx), :]
    f = wgs[0].shape[0]
    for q in range(4):
        outs[q][...] = out_s[rows_at(col ^ q, u), :]
        wgs[q][...] = wg_s[rows_at(col ^ q, f), :]


def spread(side_of, slot, a_side, g_ref, acc):
    r, c, x = position()
    n, slots_n, tile, _ = a_side.shape
    lane = lax.rem(r * 4 * n, LANES) + (2 * c + side_of(x)) * n
    for t in range(n):
        g = g_ref[:, t * tile : (t + 1) * tile]
        for k in range(0, slots_n, 2):
            right = jnp.concatenate([a_side[t, k], a_side[t, k + 1]], axis=1)
            part = jnp.dot(g, right, preferred_element_type=F32)
            acc[slot[k, lane + t]] += part[:, :tile]
            acc[slot[k + 1, lane + t]] += part[:, tile:]


def spread_first_kernel(side_of, slot, a_side, g_ref, acc):
    acc[...] = jnp.zeros_like(acc)
    spread(side_of, slot, a_side, g_ref, acc)


def spread_last_kernel(side_of, slot, a_side, g_ref, before, own, own_send, stay, send, acc):
    acc[...] = before[...]
    spread(side_of, slot, a_side, g_ref, acc)
    _, c, _ = position()
    f = own.shape[0]
    top, low = rows_at(c, f), rows_at(1 - c, f)
    tile = a_side.shape[3]
    blk = own.shape[1] // tile
    for d in range(send.shape[0]):
        for o in range(CAP):
            stay[d, o] = acc[blk + d * CAP + o, top, :]
            send[d, o] = acc[blk + d * CAP + o, low, :].astype(BF16)
    for b in range(blk):
        own[:, b * tile : (b + 1) * tile] = acc[b, top, :]
        own_send[:, b * tile : (b + 1) * tile] = acc[b, low, :]


def total_kernel(stay, came, w0, w1, w2, w3, out):
    f, tile = stay.shape[2], stay.shape[3]
    part = ((w0[...] + w1[...]) + (w2[...] + w3[...])).astype(BF16)
    for d in range(stay.shape[0]):
        for o in range(CAP):
            out[d, o * f : (o + 1) * f, :] = (stay[d, o] + came[d, o].astype(F32)).astype(BF16)
        for h in range(part.shape[1] // tile):
            at = (CAP + h) * f
            out[d, at : at + f, :] = part[:, h * tile : (h + 1) * tile]


def collect_kernel(scale, sel, own, came, back, out, wg):
    tile = back.shape[2]
    f = own.shape[0]
    out[...] = own[...] + came[...]
    for d in range(back.shape[0]):
        for o in range(CAP):
            term = back[d, o * f : (o + 1) * f, :].astype(F32)
            out[:, rows_at(sel[o, d], tile)] += term
    for h in range(wg.shape[1] // tile):
        at = (CAP + h) * f
        total = back[0, at : at + f, :].astype(F32)
        for d in range(1, back.shape[0]):
            total = total + back[d, at : at + f, :].astype(F32)
        wg[:, h * tile : (h + 1) * tile] = total * scale


def place_kernel(p0, p1, p2, p3, out):
    _, c, x = position()
    width = p0.shape[1]
    for q, piece in enumerate((p0, p1, p2, p3)):
        out[:, rows_at((c ^ (q & 1)) * 2 + (x ^ (q >> 1)), width)] = piece[...]


def layer(feats_t, adj_index, adj_weight, weight, cotangent_t):
    f, nodes = feats_t.shape
    blk, slots_n, tile, _ = adj_weight.shape
    units_loc = cotangent_t.shape[0]
    f_in, units = weight.shape
    rows_n, cols_n = lax.axis_size("rows"), lax.axis_size("cols")
    assert cols_n == 4 and rows_n & (rows_n - 1) == 0 and blk % 4 == 0
    table_n = blk + rows_n * CAP
    fx = 2 * f
    quarter = nodes // 4
    big = min(48, 8 + rows_n)

    def mate(v, q):
        return lax.ppermute(v, "cols", [(i, i ^ q) for i in range(cols_n)])

    def over_rows(v):
        return lax.all_to_all(v, "rows", 0, 0, tiled=True)

    adj_t = adj_index.T
    in_hbm = functools.partial(pltpu.with_memory_space_constraint, memory_space=pltpu.HBM)
    part = (rows_n, CAP, f, tile)
    piece = ((units_loc, quarter), BF16)
    sel, feats, adj, sends = call(
        choose_kernel, [HBM, HBM],
        [((8, LANES), I32), ((f, nodes), BF16), (adj_t.shape, I32), (part, BF16)],
        [in_hbm(adj_t), in_hbm(feats_t)],
        [pltpu.SMEM((8, LANES), I32), pltpu.SemaphoreType.DMA((3,))], mib=big,
    )
    feats_mate = mate(feats, 1)
    got = over_rows(sends)

    def far(x):
        return 1 - x

    def near(x):
        return x

    a_side = ((blk // 4, slots_n, tile, tile), BF16)
    sems = [pltpu.SemaphoreType.DMA((4 + blk // 4,))]
    a_far, *cots = call(
        functools.partial(fetch_kernel, far), [HBM, HBM], [a_side] + [piece] * 4,
        [in_hbm(adj_weight), in_hbm(cotangent_t)], sems,
    )
    a_near = call(
        functools.partial(fetch_kernel, near), [HBM], a_side,
        [in_hbm(adj_weight)], sems,
    )
    slot = call(
        functools.partial(slot_kernel, blk), [VMEM],
        ((slots_n, LANES), I32), [adj], mib=big,
    )
    cots = [cots[0]] + [mate(cots[q], q) for q in (1, 2, 3)]
    got_mate = mate(got, 1)

    a_flops = blk // 2 * slots_n * fx * tile * tile

    def gather(side_of, a_side):
        args = [slot, a_side, feats, feats_mate, got, got_mate]
        return call(
            functools.partial(gather_kernel, side_of), [SMEM] + [VMEM] * (len(args) - 1),
            ((fx, quarter), BF16), args, [pltpu.VMEM((table_n, fx, tile), BF16)], a_flops,
            big,
        )

    agg_far = gather(far, a_far)
    agg_came = mate(agg_far, 2)
    agg_near = gather(near, a_near)

    half_g = ((fx, quarter), BF16)
    wg_part = ((f, units), F32)
    args = [agg_near, agg_came, weight, *cots]
    *outs, g_send, g_keep, w0, w1, w2, w3 = call(
        dense_kernel, [VMEM] * len(args),
        [piece] * 4 + [half_g] * 2 + [wg_part] * 4, args,
        [
            pltpu.VMEM((f_in, quarter), BF16),
            pltpu.VMEM((units, quarter), BF16),
            pltpu.VMEM((units, quarter), BF16),
            pltpu.VMEM((f_in, quarter), BF16),
            pltpu.VMEM((f_in, units), F32),
        ],
        6 * f_in * units * quarter, 12,
    )
    g_came = mate(g_send, 2)
    wgs = [w0, mate(w1, 1), mate(w2, 2), mate(w3, 3)]

    acc = call(
        functools.partial(spread_first_kernel, near), [SMEM, VMEM, VMEM],
        ((table_n, fx, tile), F32), [slot, a_near, g_keep], [], a_flops, big,
    )
    own, own_send, stay, send = call(
        functools.partial(spread_last_kernel, far), [SMEM, VMEM, VMEM, VMEM],
        [((f, nodes), F32)] * 2 + [(part, F32), (part, BF16)],
        [slot, a_far, g_came, acc], [pltpu.VMEM((table_n, fx, tile), F32)], a_flops, big + 8,
    )
    own_came = mate(own_send, 1)
    total = call(
        total_kernel, [VMEM] * 6, ((rows_n, CAP * f + f * units // tile, tile), BF16),
        [stay, mate(send, 1), *wgs], mib=big,
    )
    feat_grad, weight_grad = call(
        functools.partial(collect_kernel, 1.0 / math.sqrt(nodes * rows_n)),
        [SMEM, VMEM, VMEM, VMEM], [((f, nodes), F32), wg_part],
        [sel, own, own_came, over_rows(total)], mib=big, out=True,
    )

    outs = [outs[0]] + [mate(outs[q], q) for q in (1, 2, 3)]
    output_t = call(place_kernel, [VMEM] * 4, ((units_loc, nodes), BF16), outs, out=True)
    return output_t, weight_grad, feat_grad


def solution(mesh):
    return jax.shard_map(
        layer,
        mesh=mesh,
        in_specs=(P("cols", "rows"), P(), P("rows", None, None, None), P(), P("cols", "rows")),
        out_specs=(P("cols", "rows"), P("cols", None), P("cols", "rows")),
        check_vma=False,
    )
```

```python
import functools
import math

import jax
import jax.numpy as jnp
from jax import lax
from jax.experimental import pallas as pl
from jax.experimental.pallas import tpu as pltpu
from jax.sharding import PartitionSpec as P

CAP = 4
LANES = 128
F32, BF16, I32 = jnp.float32, jnp.bfloat16, jnp.int32
VMEM = pl.BlockSpec(memory_space=pltpu.VMEM)
SMEM = pl.BlockSpec(memory_space=pltpu.SMEM)
HBM = pl.BlockSpec(memory_space=pltpu.HBM)
MIB = 1 << 20


def call(kernel, in_specs, outs, args, scratch=(), flops=10**6, mib=8):
    kinds = {"vmem": (pltpu.VMEM, VMEM), "smem": (pltpu.SMEM, SMEM)}
    shapes = [kinds[k][0](s, d) if k in kinds else jax.ShapeDtypeStruct(s, d) for k, s, d in outs]
    specs = [kinds[k][1] if k in kinds else {"hbm": HBM, "out": VMEM}[k] for k, _, _ in outs]
    nbytes = sum(a.size * a.dtype.itemsize for a in args)
    result = pl.pallas_call(
        kernel,
        out_shape=shapes,
        in_specs=in_specs,
        out_specs=specs,
        scratch_shapes=list(scratch),
        compiler_params=pltpu.CompilerParams(vmem_limit_bytes=mib * MIB),
        cost_estimate=pl.CostEstimate(flops=flops, bytes_accessed=nbytes, transcendentals=0),
    )(*args)
    return result if len(outs) > 1 else result[0]


def iota(shape, dim):
    return lax.broadcasted_iota(I32, shape, dim)


def position():
    col = lax.axis_index("cols")
    return lax.axis_index("rows"), lax.rem(col, 2), col // 2


def rows_at(start, size):
    return pl.ds(pl.multiple_of(start * size, size), size)


def choose_kernel(adj_hbm, feats, sel, copied, adj_ref, sends, sems):
    names = pltpu.make_async_copy(adj_hbm, adj_ref, sems.at[0])
    names.start()
    copy = pltpu.make_async_copy(feats, copied, sems.at[1])
    copy.start()
    slots_n, ids_n = adj_ref.shape
    tile = sends.shape[3]
    blk = feats.shape[1] // tile
    r, _, _ = position()
    mine = r * blk + iota((blk, ids_n), 0)
    group = (iota((ids_n, LANES), 0) // blk == iota((ids_n, LANES), 1)).astype(BF16)
    below = (iota((blk, blk), 1) < iota((blk, blk), 0)).astype(BF16)
    number = iota((blk, LANES), 0).astype(F32)
    names.wait()
    adj = adj_ref[...]
    hits = jnp.zeros((blk, ids_n), F32)
    for k in range(slots_n):
        hits += (adj[k : k + 1, :] == mine).astype(F32)
    wants = jnp.dot(hits.astype(BF16), group, preferred_element_type=F32) > 0.5
    order = jnp.dot(below, wants.astype(BF16), preferred_element_type=F32)
    picks = []
    for o in range(CAP):
        pick = jnp.where(wants & (jnp.abs(order - o) < 0.5), number, 0.0)
        picks.append(jnp.sum(pick, axis=0, keepdims=True).astype(I32))
    copy.wait()
    for d in range(sends.shape[0]):
        for o in range(CAP):
            at = picks[o][0, d]
            sel[o, d] = at
            source = copied.at[:, rows_at(at, tile)]
            pltpu.make_async_copy(source, sends.at[d, o], sems.at[2]).start()
    pltpu.make_async_copy(sends, sends, sems.at[2]).wait()


def slot_kernel(blk, adj_ref, slots, out_ref, sem):
    slots_n, ids_n = adj_ref.shape
    r, _, _ = position()
    start = pl.multiple_of((r * blk) // LANES * LANES, LANES)
    near = adj_ref[:, pl.ds(start, LANES)]
    block = iota((ids_n, LANES), 0)
    seen = jnp.zeros((ids_n, LANES), F32)
    for k in range(slots_n):
        seen += (near[k : k + 1, :] == block).astype(F32)
    own = ((iota((LANES, LANES), 0) + start) // blk == r).astype(BF16)
    needed = jnp.dot(seen.astype(BF16), own, preferred_element_type=F32) > 0.5
    a, b = iota((ids_n, ids_n), 0), iota((ids_n, ids_n), 1)
    earlier = ((b < a) & (a // blk == b // blk)).astype(BF16)
    place = jnp.dot(earlier, needed.astype(BF16), preferred_element_type=F32).astype(I32)
    source = block // blk
    slot = jnp.where(source == r, block % blk, blk + source * CAP + place).astype(F32)
    for k in range(slots_n):
        found = jnp.where(near[k : k + 1, :] == block, slot, 0.0)
        out_ref[k : k + 1, :] = jnp.sum(found, axis=0, keepdims=True).astype(I32)
    copy = pltpu.make_async_copy(out_ref, slots, sem)
    copy.start()
    copy.wait()


def fetch_kernel(side_of, a_hbm, *rest):
    _, c, x = position()
    copies = []
    if len(rest) > 2:
        cot, a_side, *pieces, sems = rest
        width = pieces[0].shape[1]
        for q in (1, 2, 3, 0):
            at = rows_at((c ^ (q & 1)) * 2 + (x ^ (q >> 1)), width)
            copies.append(pltpu.make_async_copy(cot.at[:, at], pieces[q], sems.at[q]))
    else:
        a_side, sems = rest
    n = a_side.shape[0]
    first = (2 * c + side_of(x)) * n
    for i in range(n):
        copies.append(pltpu.make_async_copy(a_hbm.at[first + i], a_side.at[i], sems.at[4 + i]))
    for copy in copies:
        copy.start()
    for copy in copies:
        copy.wait()


def gather_kernel(side_of, slot, a_side, mine, mate, got, got_mate, out, table):
    r, c, x = position()
    f = mine.shape[0]
    top, low = rows_at(c, f), rows_at(1 - c, f)
    tile = a_side.shape[3]
    blk = mine.shape[1] // tile
    for b in range(blk):
        table[b, top, :] = mine[:, b * tile : (b + 1) * tile]
        table[b, low, :] = mate[:, b * tile : (b + 1) * tile]
    for d in range(got.shape[0]):
        for o in range(CAP):
            table[blk + d * CAP + o, top, :] = got[d, o]
            table[blk + d * CAP + o, low, :] = got_mate[d, o]
    n, slots_n, tile, _ = a_side.shape
    lane = lax.rem(r * 4 * n, LANES) + (2 * c + side_of(x)) * n
    for t in range(n):
        acc = None
        for k in range(0, slots_n, 2):
            left = [table[slot[k + h, lane + t]] for h in range(2)]
            right = [a_side[t, k + h] for h in range(2)]
            part = lax.dot_general(
                jnp.concatenate(left, axis=1),
                jnp.concatenate(right, axis=1),
                (((1,), (1,)), ((), ())),
                preferred_element_type=F32,
            )
            acc = part if acc is None else acc + part
        out[:, t * tile : (t + 1) * tile] = acc.astype(BF16)


def dense_kernel(keep, came, w_ref, c0, c1, c2, c3, *rest):
    outs, (g_send, g_keep, wg_send, wg_keep) = rest[:4], rest[4:8]
    agg, cot, out_s, grad_s, wg_s = rest[8:]
    _, c, x = position()
    fx = keep.shape[0]
    u = c0.shape[0]
    col = 2 * x + c
    agg[rows_at(x, fx), :] = keep[...]
    agg[rows_at(1 - x, fx), :] = came[...]
    for q, piece in enumerate((c0, c1, c2, c3)):
        cot[rows_at(col ^ q, u), :] = piece[...]
    w = w_ref[...]
    act = agg[...]
    pre_act = lax.dot_general(w, act, (((0,), (0,)), ((), ())), preferred_element_type=F32)
    sigm = jax.nn.sigmoid(pre_act)
    out_s[...] = (pre_act * sigm).astype(BF16)
    pre = (cot[...].astype(F32) * sigm * (1.0 + pre_act * (1.0 - sigm))).astype(BF16)
    grad_s[...] = jnp.dot(w, pre, preferred_element_type=F32).astype(BF16)
    wg_s[...] = lax.dot_general(act, pre, (((1,), (1,)), ((), ())), preferred_element_type=F32)
    g_keep[...] = grad_s[rows_at(x, fx), :]
    g_send[...] = grad_s[rows_at(1 - x, fx), :]
    wg_keep[...] = wg_s[rows_at(x, fx), :]
    wg_send[...] = wg_s[rows_at(1 - x, fx), :]
    for q in range(4):
        outs[q][...] = out_s[rows_at(col ^ q, u), :]


def spread(side_of, slot, a_side, g_ref, acc):
    r, c, x = position()
    n, slots_n, tile, _ = a_side.shape
    lane = lax.rem(r * 4 * n, LANES) + (2 * c + side_of(x)) * n
    for t in range(n):
        g = g_ref[:, t * tile : (t + 1) * tile]
        for k in range(0, slots_n, 2):
            right = jnp.concatenate([a_side[t, k], a_side[t, k + 1]], axis=1)
            part = jnp.dot(g, right, preferred_element_type=F32)
            acc[slot[k, lane + t]] += part[:, :tile]
            acc[slot[k + 1, lane + t]] += part[:, tile:]


def spread_first_kernel(side_of, slot, a_side, g_ref, acc):
    acc[...] = jnp.zeros_like(acc)
    spread(side_of, slot, a_side, g_ref, acc)


def spread_last_kernel(side_of, slot, a_side, g_ref, before, wg, wg_came, *rest):
    own, own_send, stay, send, wg_keep, wg_send, acc = rest
    acc[...] = before[...]
    spread(side_of, slot, a_side, g_ref, acc)
    _, c, _ = position()
    f = own.shape[0]
    top, low = rows_at(c, f), rows_at(1 - c, f)
    tile = a_side.shape[3]
    blk = own.shape[1] // tile
    for d in range(send.shape[0]):
        for o in range(CAP):
            stay[d, o] = acc[blk + d * CAP + o, top, :]
            send[d, o] = acc[blk + d * CAP + o, low, :].astype(BF16)
    for b in range(blk):
        own[:, b * tile : (b + 1) * tile] = acc[b, top, :]
        own_send[:, b * tile : (b + 1) * tile] = acc[b, low, :]
    wg_keep[...] = wg[top, :] + wg_came[top, :]
    wg_send[...] = wg[low, :] + wg_came[low, :]


def total_kernel(stay, came, wg, wg_came, out, packed, sems):
    f, tile = stay.shape[2], stay.shape[3]
    part = (wg[...] + wg_came[...]).astype(BF16)
    copies = []
    for d in range(stay.shape[0]):
        for o in range(CAP):
            packed[d, o * f : (o + 1) * f, :] = (stay[d, o] + came[d, o].astype(F32)).astype(BF16)
        for h in range(part.shape[1] // tile):
            at = (CAP + h) * f
            packed[d, at : at + f, :] = part[:, h * tile : (h + 1) * tile]
        copies.append(pltpu.make_async_copy(packed.at[d], out.at[d], sems.at[d]))
        copies[-1].start()
    for copy in copies:
        copy.wait()


def collect_kernel(scale, sel, own, came, back, out, wg_out, acc, wg, sems):
    tile = back.shape[2]
    f = own.shape[0]
    half = f // 2
    copies = []
    for h in range(2):
        rows = slice(h * half, (h + 1) * half)
        acc[rows, :] = own[rows, :] + came[rows, :]
        for d in range(back.shape[0]):
            for o in range(CAP):
                term = back[d, o * f + h * half : o * f + (h + 1) * half, :].astype(F32)
                acc[rows, rows_at(sel[o, d], tile)] += term
        copies.append(pltpu.make_async_copy(acc.at[rows, :], out.at[rows, :], sems.at[h]))
        copies[-1].start()
    for h in range(wg.shape[1] // tile):
        at = (CAP + h) * f
        total = back[0, at : at + f, :].astype(F32)
        for d in range(1, back.shape[0]):
            total = total + back[d, at : at + f, :].astype(F32)
        wg[:, h * tile : (h + 1) * tile] = total * scale
    copies.append(pltpu.make_async_copy(wg, wg_out, sems.at[2]))
    copies[-1].start()
    for copy in copies:
        copy.wait()


def place_kernel(p0, p1, p2, p3, out):
    _, c, x = position()
    width = p0.shape[1]
    for q, piece in enumerate((p0, p1, p2, p3)):
        out[:, rows_at((c ^ (q & 1)) * 2 + (x ^ (q >> 1)), width)] = piece[...]


def layer(feats_t, adj_index, adj_weight, weight, cotangent_t):
    f, nodes = feats_t.shape
    blk, slots_n, tile, _ = adj_weight.shape
    units_loc = cotangent_t.shape[0]
    f_in, units = weight.shape
    rows_n, cols_n = lax.axis_size("rows"), lax.axis_size("cols")
    assert cols_n == 4 and rows_n & (rows_n - 1) == 0 and blk % 4 == 0
    table_n = blk + rows_n * CAP
    fx = 2 * f
    quarter = nodes // 4
    big = min(48, 8 + rows_n)

    def mate(v, q):
        return lax.ppermute(v, "cols", [(i, i ^ q) for i in range(cols_n)])

    def over_rows(v):
        return lax.all_to_all(v, "rows", 0, 0, tiled=True)

    adj_t = adj_index.T
    in_hbm = functools.partial(pltpu.with_memory_space_constraint, memory_space=pltpu.HBM)
    part = (rows_n, CAP, f, tile)
    piece = ("vmem", (units_loc, quarter), BF16)
    sel, feats, adj, sends = call(
        choose_kernel, [HBM, HBM],
        [("smem", (CAP, rows_n), I32), ("vmem", (f, nodes), BF16), ("vmem", adj_t.shape, I32),
         ("hbm", part, BF16)],
        [in_hbm(adj_t), in_hbm(feats_t)], [pltpu.SemaphoreType.DMA((3,))], mib=big,
    )
    feats_mate = mate(feats, 1)
    got = over_rows(sends)

    def far(x):
        return 1 - x

    def near(x):
        return x

    a_side = ("vmem", (blk // 4, slots_n, tile, tile), BF16)
    sems = [pltpu.SemaphoreType.DMA((4 + blk // 4,))]
    a_far, *cots = call(
        functools.partial(fetch_kernel, far), [HBM, HBM], [a_side] + [piece] * 4,
        [in_hbm(adj_weight), in_hbm(cotangent_t)], sems,
    )
    a_near = call(
        functools.partial(fetch_kernel, near), [HBM], [a_side],
        [in_hbm(adj_weight)], sems,
    )
    slot = call(
        functools.partial(slot_kernel, blk), [VMEM],
        [("smem", (slots_n, LANES), I32)], [adj],
        [pltpu.VMEM((slots_n, LANES), I32), pltpu.SemaphoreType.DMA], mib=big,
    )
    cots = [cots[0]] + [mate(cots[q], q) for q in (1, 2, 3)]
    got_mate = mate(got, 1)

    a_flops = blk // 2 * slots_n * fx * tile * tile

    half_g = ("vmem", (fx, quarter), BF16)

    def gather(side_of, a_side):
        args = [slot, a_side, feats, feats_mate, got, got_mate]
        return call(
            functools.partial(gather_kernel, side_of), [SMEM] + [VMEM] * (len(args) - 1),
            [half_g], args, [pltpu.VMEM((table_n, fx, tile), BF16)], a_flops,
            big,
        )

    agg_far = gather(far, a_far)
    agg_came = mate(agg_far, 2)
    agg_near = gather(near, a_near)

    args = [agg_near, agg_came, weight, *cots]
    *outs, g_send, g_keep, wg_send, wg_keep = call(
        dense_kernel, [VMEM] * len(args),
        [piece] * 4 + [half_g] * 2 + [("vmem", (fx, units), F32)] * 2, args,
        [
            pltpu.VMEM((f_in, quarter), BF16),
            pltpu.VMEM((units, quarter), BF16),
            pltpu.VMEM((units, quarter), BF16),
            pltpu.VMEM((f_in, quarter), BF16),
            pltpu.VMEM((f_in, units), F32),
        ],
        6 * f_in * units * quarter, 12,
    )
    g_came = mate(g_send, 2)
    wg_came = mate(wg_send, 2)

    acc = call(
        functools.partial(spread_first_kernel, near), [SMEM, VMEM, VMEM],
        [("vmem", (table_n, fx, tile), F32)], [slot, a_near, g_keep], [], a_flops, big,
    )
    wg_part = ((f, units), F32)
    own, own_send, stay, send, wg_keep, wg_send = call(
        functools.partial(spread_last_kernel, far), [SMEM] + [VMEM] * 5,
        [("vmem", (f, nodes), F32)] * 2
        + [("vmem", part, F32), ("vmem", part, BF16)]
        + [("vmem", *wg_part)] * 2,
        [slot, a_far, g_came, acc, wg_keep, wg_came],
        [pltpu.VMEM((table_n, fx, tile), F32)], a_flops, big + 8,
    )
    packed = ((rows_n, CAP * f + f * units // tile, tile), BF16)
    total = call(
        total_kernel, [VMEM] * 4, [("hbm", *packed)],
        [stay, mate(send, 1), wg_keep, mate(wg_send, 1)],
        [pltpu.VMEM(*packed), pltpu.SemaphoreType.DMA((rows_n,))], mib=big,
    )
    back = over_rows(total)
    own_came = mate(own_send, 1)
    feat_grad, weight_grad = call(
        functools.partial(collect_kernel, 1.0 / math.sqrt(nodes * rows_n)),
        [SMEM, VMEM, VMEM, VMEM], [("hbm", (f, nodes), F32), ("hbm", *wg_part)],
        [sel, own, own_came, back],
        [pltpu.VMEM((f, nodes), F32), pltpu.VMEM(*wg_part), pltpu.SemaphoreType.DMA((3,))],
        mib=big,
    )

    outs = [outs[0]] + [mate(outs[q], q) for q in (1, 2, 3)]
    output_t = call(place_kernel, [VMEM] * 4, [("out", (units_loc, nodes), BF16)], outs)
    return output_t, weight_grad, feat_grad


def solution(mesh):
    return jax.shard_map(
        layer,
        mesh=mesh,
        in_specs=(P("cols", "rows"), P(), P("rows", None, None, None), P(), P("cols", "rows")),
        out_specs=(P("cols", "rows"), P("cols", None), P("cols", "rows")),
        check_vma=False,
    )
```

```python
import functools
import math

import jax
import jax.numpy as jnp
from jax import lax
from jax.experimental import pallas as pl
from jax.experimental.pallas import tpu as pltpu
from jax.sharding import PartitionSpec as P

CAP = 4
LANES = 128
F32, BF16, I32 = jnp.float32, jnp.bfloat16, jnp.int32
VMEM = pl.BlockSpec(memory_space=pltpu.VMEM)
SMEM = pl.BlockSpec(memory_space=pltpu.SMEM)
HBM = pl.BlockSpec(memory_space=pltpu.HBM)
MIB = 1 << 20


def order_of(rows_n):
    bits = (rows_n // 2).bit_length() - 1
    order = []
    for i in range(rows_n // 2):
        gray = i ^ (i >> 1)
        at = sum(((gray >> b) & 1) << (bits - 1 - b) for b in range(bits)) + rows_n // 2
        order += [at, rows_n - 1 - at]
    return order


def call(kernel, in_specs, outs, args, scratch=(), flops=10**6, mib=8):
    kinds = {"vmem": (pltpu.VMEM, VMEM), "smem": (pltpu.SMEM, SMEM)}
    shapes = [kinds[k][0](s, d) if k in kinds else jax.ShapeDtypeStruct(s, d) for k, s, d in outs]
    specs = [kinds[k][1] if k in kinds else {"hbm": HBM, "out": VMEM}[k] for k, _, _ in outs]
    nbytes = sum(a.size * a.dtype.itemsize for a in args)
    result = pl.pallas_call(
        kernel,
        out_shape=shapes,
        in_specs=in_specs,
        out_specs=specs,
        scratch_shapes=list(scratch),
        compiler_params=pltpu.CompilerParams(vmem_limit_bytes=mib * MIB),
        cost_estimate=pl.CostEstimate(flops=flops, bytes_accessed=nbytes, transcendentals=0),
    )(*args)
    return result if len(outs) > 1 else result[0]


def iota(shape, dim):
    return lax.broadcasted_iota(I32, shape, dim)


def position():
    col = lax.axis_index("cols")
    return lax.axis_index("rows"), lax.rem(col, 2), col // 2


def rows_at(start, size):
    return pl.ds(pl.multiple_of(start * size, size), size)


def choose_kernel(order, adj_hbm, feats, sel, copied, adj_ref, sends, sems):
    names = pltpu.make_async_copy(adj_hbm, adj_ref, sems.at[0])
    names.start()
    copy = pltpu.make_async_copy(feats, copied, sems.at[1])
    copy.start()
    slots_n, ids_n = adj_ref.shape
    tile = sends.shape[3]
    blk = feats.shape[1] // tile
    r, _, _ = position()
    mine = r * blk + iota((blk, ids_n), 0)
    group = (iota((ids_n, LANES), 0) // blk == iota((ids_n, LANES), 1)).astype(BF16)
    below = (iota((blk, blk), 1) < iota((blk, blk), 0)).astype(BF16)
    number = iota((blk, LANES), 0).astype(F32)
    names.wait()
    adj = adj_ref[...]
    hits = jnp.zeros((blk, ids_n), F32)
    for k in range(slots_n):
        hits += (adj[k : k + 1, :] == mine).astype(F32)
    wants = jnp.dot(hits.astype(BF16), group, preferred_element_type=F32) > 0.5
    rank = jnp.dot(below, wants.astype(BF16), preferred_element_type=F32)
    picks = []
    for o in range(CAP):
        pick = jnp.where(wants & (jnp.abs(rank - o) < 0.5), number, 0.0)
        picks.append(jnp.sum(pick, axis=0, keepdims=True).astype(I32))
    copy.wait()
    for p, d in enumerate(order):
        for o in range(CAP):
            at = picks[o][0, d]
            sel[o, p] = at
            source = copied.at[:, rows_at(at, tile)]
            pltpu.make_async_copy(source, sends.at[p, o], sems.at[2]).start()
    pltpu.make_async_copy(sends, sends, sems.at[2]).wait()


def slot_kernel(order, blk, adj_ref, slots, out_ref, sem):
    slots_n, ids_n = adj_ref.shape
    r, _, _ = position()
    start = pl.multiple_of((r * blk) // LANES * LANES, LANES)
    near = adj_ref[:, pl.ds(start, LANES)]
    block = iota((ids_n, LANES), 0)
    seen = jnp.zeros((ids_n, LANES), F32)
    for k in range(slots_n):
        seen += (near[k : k + 1, :] == block).astype(F32)
    own = ((iota((LANES, LANES), 0) + start) // blk == r).astype(BF16)
    needed = jnp.dot(seen.astype(BF16), own, preferred_element_type=F32) > 0.5
    a, b = iota((ids_n, ids_n), 0), iota((ids_n, ids_n), 1)
    earlier = ((b < a) & (a // blk == b // blk)).astype(BF16)
    place = jnp.dot(earlier, needed.astype(BF16), preferred_element_type=F32).astype(I32)
    turn = [jnp.full((blk, LANES), order.index(d), I32) for d in range(len(order))]
    remote = blk + jnp.concatenate(turn, axis=0) * CAP + place
    slot = jnp.where(block // blk == r, block % blk, remote).astype(F32)
    for k in range(slots_n):
        found = jnp.where(near[k : k + 1, :] == block, slot, 0.0)
        out_ref[k : k + 1, :] = jnp.sum(found, axis=0, keepdims=True).astype(I32)
    copy = pltpu.make_async_copy(out_ref, slots, sem)
    copy.start()
    copy.wait()


def fetch_kernel(side_of, a_hbm, *rest):
    _, c, x = position()
    copies = []
    if len(rest) > 2:
        cot, a_side, *pieces, sems = rest
        width = pieces[0].shape[1]
        for q in (1, 2, 3, 0):
            at = rows_at((c ^ (q & 1)) * 2 + (x ^ (q >> 1)), width)
            copies.append(pltpu.make_async_copy(cot.at[:, at], pieces[q], sems.at[q]))
    else:
        a_side, sems = rest
    n = a_side.shape[0]
    first = (2 * c + side_of(x)) * n
    for i in range(n):
        copies.append(pltpu.make_async_copy(a_hbm.at[first + i], a_side.at[i], sems.at[4 + i]))
    for copy in copies:
        copy.start()
    for copy in copies:
        copy.wait()


def gather_kernel(side_of, slot, a_side, mine, mate, got, got_mate, out, table):
    r, c, x = position()
    f = mine.shape[0]
    top, low = rows_at(c, f), rows_at(1 - c, f)
    tile = a_side.shape[3]
    blk = mine.shape[1] // tile
    for b in range(blk):
        table[b, top, :] = mine[:, b * tile : (b + 1) * tile]
        table[b, low, :] = mate[:, b * tile : (b + 1) * tile]
    for d in range(got.shape[0]):
        for o in range(CAP):
            table[blk + d * CAP + o, top, :] = got[d, o]
            table[blk + d * CAP + o, low, :] = got_mate[d, o]
    n, slots_n, tile, _ = a_side.shape
    lane = lax.rem(r * 4 * n, LANES) + (2 * c + side_of(x)) * n
    for t in range(n):
        acc = None
        for k in range(0, slots_n, 2):
            left = [table[slot[k + h, lane + t]] for h in range(2)]
            right = [a_side[t, k + h] for h in range(2)]
            part = lax.dot_general(
                jnp.concatenate(left, axis=1),
                jnp.concatenate(right, axis=1),
                (((1,), (1,)), ((), ())),
                preferred_element_type=F32,
            )
            acc = part if acc is None else acc + part
        out[:, t * tile : (t + 1) * tile] = acc.astype(BF16)


def dense_kernel(keep, came, w_ref, c0, c1, c2, c3, *rest):
    outs, (g_send, g_keep, wg_send, wg_keep) = rest[:4], rest[4:8]
    agg, cot, out_s, grad_s, wg_s = rest[8:]
    _, c, x = position()
    fx = keep.shape[0]
    u = c0.shape[0]
    col = 2 * x + c
    agg[rows_at(x, fx), :] = keep[...]
    agg[rows_at(1 - x, fx), :] = came[...]
    for q, piece in enumerate((c0, c1, c2, c3)):
        cot[rows_at(col ^ q, u), :] = piece[...]
    w = w_ref[...]
    act = agg[...]
    pre_act = lax.dot_general(w, act, (((0,), (0,)), ((), ())), preferred_element_type=F32)
    sigm = jax.nn.sigmoid(pre_act)
    out_s[...] = (pre_act * sigm).astype(BF16)
    pre = (cot[...].astype(F32) * sigm * (1.0 + pre_act * (1.0 - sigm))).astype(BF16)
    grad_s[...] = jnp.dot(w, pre, preferred_element_type=F32).astype(BF16)
    wg_s[...] = lax.dot_general(act, pre, (((1,), (1,)), ((), ())), preferred_element_type=F32)
    g_keep[...] = grad_s[rows_at(x, fx), :]
    g_send[...] = grad_s[rows_at(1 - x, fx), :]
    f = fx // 2
    for h in range(2):
        wg_keep[h * f : (h + 1) * f, :] = wg_s[rows_at(2 * h + c, f), :]
        wg_send[h * f : (h + 1) * f, :] = wg_s[rows_at(2 * h + 1 - c, f), :]
    for q in range(4):
        outs[q][...] = out_s[rows_at(col ^ q, u), :]


def wg_kernel(mine, came, keep, send):
    _, _, x = position()
    f = keep.shape[0]
    keep[...] = mine[rows_at(x, f), :] + came[rows_at(x, f), :]
    send[...] = mine[rows_at(1 - x, f), :] + came[rows_at(1 - x, f), :]


def spread(side_of, slot, a_side, g_ref, acc):
    r, c, x = position()
    n, slots_n, tile, _ = a_side.shape
    lane = lax.rem(r * 4 * n, LANES) + (2 * c + side_of(x)) * n
    for t in range(n):
        g = g_ref[:, t * tile : (t + 1) * tile]
        for k in range(0, slots_n, 2):
            right = jnp.concatenate([a_side[t, k], a_side[t, k + 1]], axis=1)
            part = jnp.dot(g, right, preferred_element_type=F32)
            acc[slot[k, lane + t]] += part[:, :tile]
            acc[slot[k + 1, lane + t]] += part[:, tile:]


def spread_first_kernel(side_of, slot, a_side, g_ref, acc):
    acc[...] = jnp.zeros_like(acc)
    spread(side_of, slot, a_side, g_ref, acc)


def spread_last_kernel(side_of, slot, a_side, g_ref, before, own, own_send, stay, send, acc):
    acc[...] = before[...]
    spread(side_of, slot, a_side, g_ref, acc)
    _, c, _ = position()
    f = own.shape[0]
    top, low = rows_at(c, f), rows_at(1 - c, f)
    tile = a_side.shape[3]
    blk = own.shape[1] // tile
    for d in range(send.shape[0]):
        for o in range(CAP):
            stay[d, o] = acc[blk + d * CAP + o, top, :]
            send[d, o] = acc[blk + d * CAP + o, low, :].astype(BF16)
    for b in range(blk):
        own[:, b * tile : (b + 1) * tile] = acc[b, top, :]
        own_send[:, b * tile : (b + 1) * tile] = acc[b, low, :]


def total_kernel(stay, came, wg, wg_came, out, packed, sems):
    f, tile = stay.shape[2], stay.shape[3]
    part = (wg[...] + wg_came[...]).astype(BF16)
    copies = []
    for d in range(stay.shape[0]):
        for o in range(CAP):
            packed[d, o * f : (o + 1) * f, :] = (stay[d, o] + came[d, o].astype(F32)).astype(BF16)
        for h in range(part.shape[1] // tile):
            at = (CAP + h) * f
            packed[d, at : at + f, :] = part[:, h * tile : (h + 1) * tile]
        copies.append(pltpu.make_async_copy(packed.at[d], out.at[d], sems.at[d]))
        copies[-1].start()
    for copy in copies:
        copy.wait()


def collect_kernel(scale, sel, own, came, back, out, wg_out, acc, wg, sems):
    tile = back.shape[2]
    f = own.shape[0]
    half = f // 2
    copies = []
    for h in range(2):
        rows = slice(h * half, (h + 1) * half)
        acc[rows, :] = own[rows, :] + came[rows, :]
        for p in range(back.shape[0]):
            for o in range(CAP):
                term = back[p, o * f + h * half : o * f + (h + 1) * half, :].astype(F32)
                acc[rows, rows_at(sel[o, p], tile)] += term
        copies.append(pltpu.make_async_copy(acc.at[rows, :], out.at[rows, :], sems.at[h]))
        copies[-1].start()
    for h in range(wg.shape[1] // tile):
        at = (CAP + h) * f
        total = back[0, at : at + f, :].astype(F32)
        for d in range(1, back.shape[0]):
            total = total + back[d, at : at + f, :].astype(F32)
        wg[:, h * tile : (h + 1) * tile] = total * scale
    copies.append(pltpu.make_async_copy(wg, wg_out, sems.at[2]))
    copies[-1].start()
    for copy in copies:
        copy.wait()


def place_kernel(p0, p1, p2, p3, out):
    _, c, x = position()
    width = p0.shape[1]
    for q, piece in enumerate((p0, p1, p2, p3)):
        out[:, rows_at((c ^ (q & 1)) * 2 + (x ^ (q >> 1)), width)] = piece[...]


def layer(feats_t, adj_index, adj_weight, weight, cotangent_t):
    f, nodes = feats_t.shape
    blk, slots_n, tile, _ = adj_weight.shape
    units_loc = cotangent_t.shape[0]
    f_in, units = weight.shape
    rows_n, cols_n = lax.axis_size("rows"), lax.axis_size("cols")
    assert cols_n == 4 and rows_n & (rows_n - 1) == 0 and blk % 4 == 0
    table_n = blk + rows_n * CAP
    fx = 2 * f
    quarter = nodes // 4
    big = min(48, 8 + rows_n)

    def mate(v, q):
        return lax.ppermute(v, "cols", [(i, i ^ q) for i in range(cols_n)])

    order = order_of(rows_n)

    def over_rows(v):
        return lax.all_to_all(v, "rows", 0, 0, tiled=True, axis_index_groups=[order])

    adj_t = adj_index.T
    in_hbm = functools.partial(pltpu.with_memory_space_constraint, memory_space=pltpu.HBM)
    part = (rows_n, CAP, f, tile)
    piece = ("vmem", (units_loc, quarter), BF16)
    sel, feats, adj, sends = call(
        functools.partial(choose_kernel, order), [HBM, HBM],
        [("smem", (CAP, rows_n), I32), ("vmem", (f, nodes), BF16), ("vmem", adj_t.shape, I32),
         ("hbm", part, BF16)],
        [in_hbm(adj_t), in_hbm(feats_t)], [pltpu.SemaphoreType.DMA((3,))], mib=big,
    )
    feats_mate = mate(feats, 1)
    got = over_rows(sends)

    def far(x):
        return 1 - x

    def near(x):
        return x

    a_side = ("vmem", (blk // 4, slots_n, tile, tile), BF16)
    sems = [pltpu.SemaphoreType.DMA((4 + blk // 4,))]
    a_far, *cots = call(
        functools.partial(fetch_kernel, far), [HBM, HBM], [a_side] + [piece] * 4,
        [in_hbm(adj_weight), in_hbm(cotangent_t)], sems,
    )
    a_near = call(
        functools.partial(fetch_kernel, near), [HBM], [a_side],
        [in_hbm(adj_weight)], sems,
    )
    slot = call(
        functools.partial(slot_kernel, order, blk), [VMEM],
        [("smem", (slots_n, LANES), I32)], [adj],
        [pltpu.VMEM((slots_n, LANES), I32), pltpu.SemaphoreType.DMA], mib=big,
    )
    cots = [cots[0]] + [mate(cots[q], q) for q in (1, 2, 3)]
    got_mate = mate(got, 1)

    a_flops = blk // 2 * slots_n * fx * tile * tile

    half_g = ("vmem", (fx, quarter), BF16)

    def gather(side_of, a_side):
        args = [slot, a_side, feats, feats_mate, got, got_mate]
        return call(
            functools.partial(gather_kernel, side_of), [SMEM] + [VMEM] * (len(args) - 1),
            [half_g], args, [pltpu.VMEM((table_n, fx, tile), BF16)], a_flops,
            big,
        )

    agg_far = gather(far, a_far)
    agg_came = mate(agg_far, 2)
    agg_near = gather(near, a_near)

    args = [agg_near, agg_came, weight, *cots]
    *outs, g_send, g_keep, wg_send, wg_keep = call(
        dense_kernel, [VMEM] * len(args),
        [piece] * 4 + [half_g] * 2 + [("vmem", (fx, units), F32)] * 2, args,
        [
            pltpu.VMEM((f_in, quarter), BF16),
            pltpu.VMEM((units, quarter), BF16),
            pltpu.VMEM((units, quarter), BF16),
            pltpu.VMEM((f_in, quarter), BF16),
            pltpu.VMEM((f_in, units), F32),
        ],
        6 * f_in * units * quarter, 12,
    )
    g_came = mate(g_send, 2)
    wg_part = ((f, units), F32)
    wg_keep, wg_send = call(
        wg_kernel, [VMEM] * 2, [("vmem", *wg_part)] * 2, [wg_keep, mate(wg_send, 1)]
    )
    wg_came = mate(wg_send, 2)

    acc = call(
        functools.partial(spread_first_kernel, near), [SMEM, VMEM, VMEM],
        [("vmem", (table_n, fx, tile), F32)], [slot, a_near, g_keep], [], a_flops, big,
    )
    own, own_send, stay, send = call(
        functools.partial(spread_last_kernel, far), [SMEM] + [VMEM] * 3,
        [("vmem", (f, nodes), F32)] * 2 + [("vmem", part, F32), ("vmem", part, BF16)],
        [slot, a_far, g_came, acc], [pltpu.VMEM((table_n, fx, tile), F32)], a_flops, big + 8,
    )
    packed = ((rows_n, CAP * f + f * units // tile, tile), BF16)
    total = call(
        total_kernel, [VMEM] * 4, [("hbm", *packed)],
        [stay, mate(send, 1), wg_keep, wg_came],
        [pltpu.VMEM(*packed), pltpu.SemaphoreType.DMA((rows_n,))], mib=big,
    )
    back = over_rows(total)
    own_came = mate(own_send, 1)
    feat_grad, weight_grad = call(
        functools.partial(collect_kernel, 1.0 / math.sqrt(nodes * rows_n)),
        [SMEM, VMEM, VMEM, VMEM], [("hbm", (f, nodes), F32), ("hbm", *wg_part)],
        [sel, own, own_came, back],
        [pltpu.VMEM((f, nodes), F32), pltpu.VMEM(*wg_part), pltpu.SemaphoreType.DMA((3,))],
        mib=big,
    )

    outs = [outs[0]] + [mate(outs[q], q) for q in (1, 2, 3)]
    output_t = call(place_kernel, [VMEM] * 4, [("out", (units_loc, nodes), BF16)], outs)
    return output_t, weight_grad, feat_grad


def solution(mesh):
    return jax.shard_map(
        layer,
        mesh=mesh,
        in_specs=(P("cols", "rows"), P(), P("rows", None, None, None), P(), P("cols", "rows")),
        out_specs=(P("cols", "rows"), P("cols", None), P("cols", "rows")),
        check_vma=False,
    )
```

```python
import functools
import math

import jax
import jax.numpy as jnp
from jax import lax
from jax.experimental import pallas as pl
from jax.experimental.pallas import tpu as pltpu
from jax.sharding import PartitionSpec as P

CAP = 4
LANES = 128
F32, BF16, I32 = jnp.float32, jnp.bfloat16, jnp.int32
VMEM = pl.BlockSpec(memory_space=pltpu.VMEM)
SMEM = pl.BlockSpec(memory_space=pltpu.SMEM)
HBM = pl.BlockSpec(memory_space=pltpu.HBM)
MIB = 1 << 20


def order_of(rows_n):
    bits = (rows_n // 2).bit_length() - 1
    order = []
    for i in range(rows_n // 2):
        gray = i ^ (i >> 1)
        at = sum(((gray >> b) & 1) << (bits - 1 - b) for b in range(bits)) + rows_n // 2
        order += [at, rows_n - 1 - at]
    return order


def back_order_of(rows_n):
    pairs = rows_n // 2
    middle = [*range(pairs // 2, pairs), *range(pairs // 2 - 1, -1, -1)]
    return [2 * i for i in middle] + [2 * i + 1 for i in middle]


def call(kernel, in_specs, outs, args, scratch=(), flops=10**6, mib=8):
    kinds = {"vmem": (pltpu.VMEM, VMEM), "smem": (pltpu.SMEM, SMEM)}
    shapes = [kinds[k][0](s, d) if k in kinds else jax.ShapeDtypeStruct(s, d) for k, s, d in outs]
    specs = [kinds[k][1] if k in kinds else {"hbm": HBM, "out": VMEM}[k] for k, _, _ in outs]
    nbytes = sum(a.size * a.dtype.itemsize for a in args)
    result = pl.pallas_call(
        kernel,
        out_shape=shapes,
        in_specs=in_specs,
        out_specs=specs,
        scratch_shapes=list(scratch),
        compiler_params=pltpu.CompilerParams(vmem_limit_bytes=mib * MIB),
        cost_estimate=pl.CostEstimate(flops=flops, bytes_accessed=nbytes, transcendentals=0),
    )(*args)
    return result if len(outs) > 1 else result[0]


def iota(shape, dim):
    return lax.broadcasted_iota(I32, shape, dim)


def position():
    col = lax.axis_index("cols")
    return lax.axis_index("rows"), lax.rem(col, 2), col // 2


def rows_at(start, size):
    return pl.ds(pl.multiple_of(start * size, size), size)


def choose_kernel(order, adj_hbm, feats, sel, copied, adj_ref, sends, sems):
    names = pltpu.make_async_copy(adj_hbm, adj_ref, sems.at[0])
    names.start()
    copy = pltpu.make_async_copy(feats, copied, sems.at[1])
    copy.start()
    slots_n, ids_n = adj_ref.shape
    tile = sends.shape[3]
    blk = feats.shape[1] // tile
    r, _, _ = position()
    mine = r * blk + iota((blk, ids_n), 0)
    group = (iota((ids_n, LANES), 0) // blk == iota((ids_n, LANES), 1)).astype(BF16)
    below = (iota((blk, blk), 1) < iota((blk, blk), 0)).astype(BF16)
    number = iota((blk, LANES), 0).astype(F32)
    names.wait()
    adj = adj_ref[...]
    hits = jnp.zeros((blk, ids_n), F32)
    for k in range(slots_n):
        hits += (adj[k : k + 1, :] == mine).astype(F32)
    wants = jnp.dot(hits.astype(BF16), group, preferred_element_type=F32) > 0.5
    rank = jnp.dot(below, wants.astype(BF16), preferred_element_type=F32)
    picks = []
    for o in range(CAP):
        pick = jnp.where(wants & (jnp.abs(rank - o) < 0.5), number, 0.0)
        picks.append(jnp.sum(pick, axis=0, keepdims=True).astype(I32))
    copy.wait()
    for p, d in enumerate(order):
        for o in range(CAP):
            at = picks[o][0, d]
            sel[o, d] = at
            source = copied.at[:, rows_at(at, tile)]
            pltpu.make_async_copy(source, sends.at[p, o], sems.at[2]).start()
    pltpu.make_async_copy(sends, sends, sems.at[2]).wait()


def slot_kernel(order, blk, adj_ref, slots, out_ref, sem):
    slots_n, ids_n = adj_ref.shape
    r, _, _ = position()
    start = pl.multiple_of((r * blk) // LANES * LANES, LANES)
    near = adj_ref[:, pl.ds(start, LANES)]
    block = iota((ids_n, LANES), 0)
    seen = jnp.zeros((ids_n, LANES), F32)
    for k in range(slots_n):
        seen += (near[k : k + 1, :] == block).astype(F32)
    own = ((iota((LANES, LANES), 0) + start) // blk == r).astype(BF16)
    needed = jnp.dot(seen.astype(BF16), own, preferred_element_type=F32) > 0.5
    a, b = iota((ids_n, ids_n), 0), iota((ids_n, ids_n), 1)
    earlier = ((b < a) & (a // blk == b // blk)).astype(BF16)
    place = jnp.dot(earlier, needed.astype(BF16), preferred_element_type=F32).astype(I32)
    turn = [jnp.full((blk, LANES), order.index(d), I32) for d in range(len(order))]
    remote = blk + jnp.concatenate(turn, axis=0) * CAP + place
    slot = jnp.where(block // blk == r, block % blk, remote).astype(F32)
    for k in range(slots_n):
        found = jnp.where(near[k : k + 1, :] == block, slot, 0.0)
        out_ref[k : k + 1, :] = jnp.sum(found, axis=0, keepdims=True).astype(I32)
    copy = pltpu.make_async_copy(out_ref, slots, sem)
    copy.start()
    copy.wait()


def fetch_kernel(side_of, a_hbm, cot, a_side, c0, c1, c2, c3, sems):
    _, c, x = position()
    pieces = (c0, c1, c2, c3)
    width = c0.shape[1]
    copies = []
    for q in (1, 2, 3, 0):
        at = rows_at((c ^ (q & 1)) * 2 + (x ^ (q >> 1)), width)
        copies.append(pltpu.make_async_copy(cot.at[:, at], pieces[q], sems.at[q]))
    n = a_side.shape[0]
    first = (2 * c + side_of(x)) * n
    for i in range(n):
        copies.append(pltpu.make_async_copy(a_hbm.at[first + i], a_side.at[i], sems.at[4 + i]))
    for copy in copies:
        copy.start()
    for copy in copies:
        copy.wait()


def gather(side_of, slot, a_side, mine, mate, got, got_mate, out, table, ready=None):
    r, c, x = position()
    f = mine.shape[0]
    top, low = rows_at(c, f), rows_at(1 - c, f)
    n, slots_n, tile, _ = a_side.shape
    blk = mine.shape[1] // tile
    for b in range(blk):
        table[b, top, :] = mine[:, b * tile : (b + 1) * tile]
        table[b, low, :] = mate[:, b * tile : (b + 1) * tile]
    for d in range(got.shape[0]):
        for o in range(CAP):
            table[blk + d * CAP + o, top, :] = got[d, o]
            table[blk + d * CAP + o, low, :] = got_mate[d, o]
    lane = lax.rem(r * 4 * n, LANES) + (2 * c + side_of(x)) * n
    for t in range(n):
        if ready is not None:
            ready[t].wait()
        acc = None
        for k in range(0, slots_n, 2):
            left = [table[slot[k + h, lane + t]] for h in range(2)]
            right = [a_side[t, k + h] for h in range(2)]
            part = lax.dot_general(
                jnp.concatenate(left, axis=1),
                jnp.concatenate(right, axis=1),
                (((1,), (1,)), ((), ())),
                preferred_element_type=F32,
            )
            acc = part if acc is None else acc + part
        out[:, t * tile : (t + 1) * tile] = acc.astype(BF16)


def gather_near_kernel(side_of, slot, a_hbm, *rest):
    mine, mate, got, got_mate, out, a_side, table, sems = rest
    _, c, x = position()
    n = a_side.shape[0]
    first = (2 * c + side_of(x)) * n
    copies = []
    for i in range(n):
        copies.append(pltpu.make_async_copy(a_hbm.at[first + i], a_side.at[i], sems.at[i]))
        copies[-1].start()
    gather(side_of, slot, a_side, mine, mate, got, got_mate, out, table, copies)


def dense_kernel(keep, came, w_ref, c0, c1, c2, c3, *rest):
    outs, (g_send, g_keep, wg_send, wg_keep) = rest[:4], rest[4:8]
    agg, cot, out_s, grad_s, wg_s = rest[8:]
    _, c, x = position()
    fx = keep.shape[0]
    u = c0.shape[0]
    col = 2 * x + c
    agg[rows_at(x, fx), :] = keep[...]
    agg[rows_at(1 - x, fx), :] = came[...]
    for q, piece in enumerate((c0, c1, c2, c3)):
        cot[rows_at(col ^ q, u), :] = piece[...]
    w = w_ref[...]
    act = agg[...]
    pre_act = lax.dot_general(w, act, (((0,), (0,)), ((), ())), preferred_element_type=F32)
    sigm = jax.nn.sigmoid(pre_act)
    out_s[...] = (pre_act * sigm).astype(BF16)
    pre = (cot[...].astype(F32) * sigm * (1.0 + pre_act * (1.0 - sigm))).astype(BF16)
    grad_s[...] = jnp.dot(w, pre, preferred_element_type=F32).astype(BF16)
    wg_s[...] = lax.dot_general(act, pre, (((1,), (1,)), ((), ())), preferred_element_type=F32)
    g_keep[...] = grad_s[rows_at(x, fx), :]
    g_send[...] = grad_s[rows_at(1 - x, fx), :]
    f = fx // 2
    for h in range(2):
        wg_keep[h * f : (h + 1) * f, :] = wg_s[rows_at(2 * h + c, f), :]
        wg_send[h * f : (h + 1) * f, :] = wg_s[rows_at(2 * h + 1 - c, f), :]
    for q in range(4):
        outs[q][...] = out_s[rows_at(col ^ q, u), :]


def wg_kernel(mine, came, keep, send):
    _, _, x = position()
    f = keep.shape[0]
    keep[...] = mine[rows_at(x, f), :] + came[rows_at(x, f), :]
    send[...] = mine[rows_at(1 - x, f), :] + came[rows_at(1 - x, f), :]


def spread(side_of, slot, a_side, g_ref, acc):
    r, c, x = position()
    n, slots_n, tile, _ = a_side.shape
    lane = lax.rem(r * 4 * n, LANES) + (2 * c + side_of(x)) * n
    for t in range(n):
        g = g_ref[:, t * tile : (t + 1) * tile]
        for k in range(0, slots_n, 2):
            right = jnp.concatenate([a_side[t, k], a_side[t, k + 1]], axis=1)
            part = jnp.dot(g, right, preferred_element_type=F32)
            acc[slot[k, lane + t]] += part[:, :tile]
            acc[slot[k + 1, lane + t]] += part[:, tile:]


def spread_first_kernel(side_of, slot, a_side, g_ref, acc):
    acc[...] = jnp.zeros_like(acc)
    spread(side_of, slot, a_side, g_ref, acc)


def spread_last_kernel(side_of, out_order, back_order, slot, a_side, g_ref, before, own, own_send, stay, send, acc):
    acc[...] = before[...]
    spread(side_of, slot, a_side, g_ref, acc)
    _, c, _ = position()
    f = own.shape[0]
    top, low = rows_at(c, f), rows_at(1 - c, f)
    tile = a_side.shape[3]
    blk = own.shape[1] // tile
    for p, d in enumerate(back_order):
        at = blk + out_order.index(d) * CAP
        for o in range(CAP):
            stay[p, o] = acc[at + o, top, :]
            send[p, o] = acc[at + o, low, :].astype(BF16)
    for b in range(blk):
        own[:, b * tile : (b + 1) * tile] = acc[b, top, :]
        own_send[:, b * tile : (b + 1) * tile] = acc[b, low, :]


def total_kernel(stay, came, wg, wg_came, out, packed, sems):
    f, tile = stay.shape[2], stay.shape[3]
    part = (wg[...] + wg_came[...]).astype(BF16)
    copies = []
    for d in range(stay.shape[0]):
        for o in range(CAP):
            packed[d, o * f : (o + 1) * f, :] = (stay[d, o] + came[d, o].astype(F32)).astype(BF16)
        for h in range(part.shape[1] // tile):
            at = (CAP + h) * f
            packed[d, at : at + f, :] = part[:, h * tile : (h + 1) * tile]
        copies.append(pltpu.make_async_copy(packed.at[d], out.at[d], sems.at[d]))
        copies[-1].start()
    for copy in copies:
        copy.wait()


def collect_kernel(scale, back_order, sel, own, came, back, out, wg_out, acc, wg, sems):
    tile = back.shape[2]
    f = own.shape[0]
    half = f // 2
    copies = []
    for h in range(2):
        rows = slice(h * half, (h + 1) * half)
        acc[rows, :] = own[rows, :] + came[rows, :]
        for p, d in enumerate(back_order):
            for o in range(CAP):
                term = back[p, o * f + h * half : o * f + (h + 1) * half, :].astype(F32)
                acc[rows, rows_at(sel[o, d], tile)] += term
        copies.append(pltpu.make_async_copy(acc.at[rows, :], out.at[rows, :], sems.at[h]))
        copies[-1].start()
    for h in range(wg.shape[1] // tile):
        at = (CAP + h) * f
        total = back[0, at : at + f, :].astype(F32)
        for d in range(1, back.shape[0]):
            total = total + back[d, at : at + f, :].astype(F32)
        wg[:, h * tile : (h + 1) * tile] = total * scale
    copies.append(pltpu.make_async_copy(wg, wg_out, sems.at[2]))
    copies[-1].start()
    for copy in copies:
        copy.wait()


def place_kernel(p0, p1, p2, p3, out):
    _, c, x = position()
    width = p0.shape[1]
    for q, piece in enumerate((p0, p1, p2, p3)):
        out[:, rows_at((c ^ (q & 1)) * 2 + (x ^ (q >> 1)), width)] = piece[...]


def layer(feats_t, adj_index, adj_weight, weight, cotangent_t):
    f, nodes = feats_t.shape
    blk, slots_n, tile, _ = adj_weight.shape
    units_loc = cotangent_t.shape[0]
    f_in, units = weight.shape
    rows_n, cols_n = lax.axis_size("rows"), lax.axis_size("cols")
    assert cols_n == 4 and rows_n & (rows_n - 1) == 0 and blk % 4 == 0
    table_n = blk + rows_n * CAP
    fx = 2 * f
    quarter = nodes // 4
    big = min(48, 8 + rows_n)

    def mate(v, q):
        return lax.ppermute(v, "cols", [(i, i ^ q) for i in range(cols_n)])

    out_order, back_order = order_of(rows_n), back_order_of(rows_n)

    def over_rows(v, order):
        return lax.all_to_all(v, "rows", 0, 0, tiled=True, axis_index_groups=[order])

    adj_t = adj_index.T
    in_hbm = functools.partial(pltpu.with_memory_space_constraint, memory_space=pltpu.HBM)
    part = (rows_n, CAP, f, tile)
    piece = ("vmem", (units_loc, quarter), BF16)
    sel, feats, adj, sends = call(
        functools.partial(choose_kernel, out_order), [HBM, HBM],
        [("smem", (CAP, rows_n), I32), ("vmem", (f, nodes), BF16), ("vmem", adj_t.shape, I32),
         ("hbm", part, BF16)],
        [in_hbm(adj_t), in_hbm(feats_t)], [pltpu.SemaphoreType.DMA((3,))], mib=big,
    )
    feats_mate = mate(feats, 1)
    got = over_rows(sends, out_order)

    def far(x):
        return 1 - x

    def near(x):
        return x

    a_side = ("vmem", (blk // 4, slots_n, tile, tile), BF16)
    sems = [pltpu.SemaphoreType.DMA((4 + blk // 4,))]
    a_far, *cots = call(
        functools.partial(fetch_kernel, far), [HBM, HBM], [a_side] + [piece] * 4,
        [in_hbm(adj_weight), in_hbm(cotangent_t)], sems,
    )
    slot = call(
        functools.partial(slot_kernel, out_order, blk), [VMEM],
        [("smem", (slots_n, LANES), I32)], [adj],
        [pltpu.VMEM((slots_n, LANES), I32), pltpu.SemaphoreType.DMA], mib=big,
    )
    cots = [cots[0]] + [mate(cots[q], q) for q in (1, 2, 3)]
    got_mate = mate(got, 1)

    a_flops = blk // 2 * slots_n * fx * tile * tile

    half_g = ("vmem", (fx, quarter), BF16)

    tables = [feats, feats_mate, got, got_mate]
    table = pltpu.VMEM((table_n, fx, tile), BF16)
    agg_far = call(
        functools.partial(gather, far), [SMEM] + [VMEM] * 5, [half_g],
        [slot, a_far, *tables], [table], a_flops, big,
    )
    agg_came = mate(agg_far, 2)
    agg_near, a_near = call(
        functools.partial(gather_near_kernel, near), [SMEM, HBM] + [VMEM] * 4,
        [half_g, a_side], [slot, in_hbm(adj_weight), *tables],
        [table, pltpu.SemaphoreType.DMA((blk // 4,))], a_flops, big,
    )

    args = [agg_near, agg_came, weight, *cots]
    *outs, g_send, g_keep, wg_send, wg_keep = call(
        dense_kernel, [VMEM] * len(args),
        [piece] * 4 + [half_g] * 2 + [("vmem", (fx, units), F32)] * 2, args,
        [
            pltpu.VMEM((f_in, quarter), BF16),
            pltpu.VMEM((units, quarter), BF16),
            pltpu.VMEM((units, quarter), BF16),
            pltpu.VMEM((f_in, quarter), BF16),
            pltpu.VMEM((f_in, units), F32),
        ],
        6 * f_in * units * quarter, 12,
    )
    g_came = mate(g_send, 2)
    wg_part = ((f, units), F32)
    wg_keep, wg_send = call(
        wg_kernel, [VMEM] * 2, [("vmem", *wg_part)] * 2, [wg_keep, mate(wg_send, 1)]
    )
    wg_came = mate(wg_send, 2)

    acc = call(
        functools.partial(spread_first_kernel, near), [SMEM, VMEM, VMEM],
        [("vmem", (table_n, fx, tile), F32)], [slot, a_near, g_keep], [], a_flops, big,
    )
    own, own_send, stay, send = call(
        functools.partial(spread_last_kernel, far, out_order, back_order), [SMEM] + [VMEM] * 3,
        [("vmem", (f, nodes), F32)] * 2 + [("vmem", part, F32), ("vmem", part, BF16)],
        [slot, a_far, g_came, acc], [pltpu.VMEM((table_n, fx, tile), F32)], a_flops, big + 8,
    )
    packed = ((rows_n, CAP * f + f * units // tile, tile), BF16)
    total = call(
        total_kernel, [VMEM] * 4, [("hbm", *packed)],
        [stay, mate(send, 1), wg_keep, wg_came],
        [pltpu.VMEM(*packed), pltpu.SemaphoreType.DMA((rows_n,))], mib=big,
    )
    back = over_rows(total, back_order)
    own_came = mate(own_send, 1)
    feat_grad, weight_grad = call(
        functools.partial(collect_kernel, 1.0 / math.sqrt(nodes * rows_n), back_order),
        [SMEM, VMEM, VMEM, VMEM], [("hbm", (f, nodes), F32), ("hbm", *wg_part)],
        [sel, own, own_came, back],
        [pltpu.VMEM((f, nodes), F32), pltpu.VMEM(*wg_part), pltpu.SemaphoreType.DMA((3,))],
        mib=big,
    )

    outs = [outs[0]] + [mate(outs[q], q) for q in (1, 2, 3)]
    output_t = call(place_kernel, [VMEM] * 4, [("out", (units_loc, nodes), BF16)], outs)
    return output_t, weight_grad, feat_grad


def solution(mesh):
    return jax.shard_map(
        layer,
        mesh=mesh,
        in_specs=(P("cols", "rows"), P(), P("rows", None, None, None), P(), P("cols", "rows")),
        out_specs=(P("cols", "rows"), P("cols", None), P("cols", "rows")),
        check_vma=False,
    )
```

```python
import functools
import math

import jax
import jax.numpy as jnp
from jax import lax
from jax.experimental import pallas as pl
from jax.experimental.pallas import tpu as pltpu
from jax.sharding import PartitionSpec as P

CAP = 4
LANES = 128
F32, BF16, I32 = jnp.float32, jnp.bfloat16, jnp.int32
VMEM = pl.BlockSpec(memory_space=pltpu.VMEM)
SMEM = pl.BlockSpec(memory_space=pltpu.SMEM)
HBM = pl.BlockSpec(memory_space=pltpu.HBM)
MIB = 1 << 20
BACK_ORDERS = {8: (4, 1, 3, 6, 2, 0, 5, 7)}


def order_of(rows_n):
    bits = (rows_n // 2).bit_length() - 1
    order = []
    for i in range(rows_n // 2):
        gray = i ^ (i >> 1)
        at = sum(((gray >> b) & 1) << (bits - 1 - b) for b in range(bits)) + rows_n // 2
        order += [at, rows_n - 1 - at]
    return order


def back_order_of(rows_n):
    if rows_n in BACK_ORDERS:
        return list(BACK_ORDERS[rows_n])
    pairs = rows_n // 2
    middle = [*range(pairs // 2, pairs), *range(pairs // 2 - 1, -1, -1)]
    return [2 * i for i in middle] + [2 * i + 1 for i in middle]


def call(kernel, in_specs, outs, args, scratch=(), flops=10**6, mib=8):
    kinds = {"vmem": (pltpu.VMEM, VMEM), "smem": (pltpu.SMEM, SMEM)}
    shapes = [kinds[k][0](s, d) if k in kinds else jax.ShapeDtypeStruct(s, d) for k, s, d in outs]
    specs = [kinds[k][1] if k in kinds else {"hbm": HBM, "out": VMEM}[k] for k, _, _ in outs]
    nbytes = sum(a.size * a.dtype.itemsize for a in args)
    result = pl.pallas_call(
        kernel,
        out_shape=shapes,
        in_specs=in_specs,
        out_specs=specs,
        scratch_shapes=list(scratch),
        compiler_params=pltpu.CompilerParams(vmem_limit_bytes=mib * MIB),
        cost_estimate=pl.CostEstimate(flops=flops, bytes_accessed=nbytes, transcendentals=0),
    )(*args)
    return result if len(outs) > 1 else result[0]


def iota(shape, dim):
    return lax.broadcasted_iota(I32, shape, dim)


def position():
    col = lax.axis_index("cols")
    return lax.axis_index("rows"), lax.rem(col, 2), col // 2


def rows_at(start, size):
    return pl.ds(pl.multiple_of(start * size, size), size)


def choose_kernel(order, adj_hbm, feats, sel, copied, adj_ref, sends, sems):
    names = pltpu.make_async_copy(adj_hbm, adj_ref, sems.at[0])
    names.start()
    copy = pltpu.make_async_copy(feats, copied, sems.at[1])
    copy.start()
    slots_n, ids_n = adj_ref.shape
    tile = sends.shape[3]
    blk = feats.shape[1] // tile
    r, _, _ = position()
    mine = r * blk + iota((blk, ids_n), 0)
    group = (iota((ids_n, LANES), 0) // blk == iota((ids_n, LANES), 1)).astype(BF16)
    below = (iota((blk, blk), 1) < iota((blk, blk), 0)).astype(BF16)
    number = iota((blk, LANES), 0).astype(F32)
    names.wait()
    adj = adj_ref[...]
    hits = jnp.zeros((blk, ids_n), F32)
    for k in range(slots_n):
        hits += (adj[k : k + 1, :] == mine).astype(F32)
    wants = jnp.dot(hits.astype(BF16), group, preferred_element_type=F32) > 0.5
    rank = jnp.dot(below, wants.astype(BF16), preferred_element_type=F32)
    picks = []
    for o in range(CAP):
        pick = jnp.where(wants & (jnp.abs(rank - o) < 0.5), number, 0.0)
        picks.append(jnp.sum(pick, axis=0, keepdims=True).astype(I32))
    copy.wait()
    for p, d in enumerate(order):
        for o in range(CAP):
            at = picks[o][0, d]
            sel[o, d] = at
            source = copied.at[:, rows_at(at, tile)]
            pltpu.make_async_copy(source, sends.at[p, o], sems.at[2]).start()
    pltpu.make_async_copy(sends, sends, sems.at[2]).wait()


def slot_kernel(order, blk, adj_ref, slots, out_ref, sem):
    slots_n, ids_n = adj_ref.shape
    r, _, _ = position()
    start = pl.multiple_of((r * blk) // LANES * LANES, LANES)
    near = adj_ref[:, pl.ds(start, LANES)]
    block = iota((ids_n, LANES), 0)
    seen = jnp.zeros((ids_n, LANES), F32)
    for k in range(slots_n):
        seen += (near[k : k + 1, :] == block).astype(F32)
    own = ((iota((LANES, LANES), 0) + start) // blk == r).astype(BF16)
    needed = jnp.dot(seen.astype(BF16), own, preferred_element_type=F32) > 0.5
    a, b = iota((ids_n, ids_n), 0), iota((ids_n, ids_n), 1)
    earlier = ((b < a) & (a // blk == b // blk)).astype(BF16)
    place = jnp.dot(earlier, needed.astype(BF16), preferred_element_type=F32).astype(I32)
    turn = [jnp.full((blk, LANES), order.index(d), I32) for d in range(len(order))]
    remote = blk + jnp.concatenate(turn, axis=0) * CAP + place
    slot = jnp.where(block // blk == r, block % blk, remote).astype(F32)
    for k in range(slots_n):
        found = jnp.where(near[k : k + 1, :] == block, slot, 0.0)
        out_ref[k : k + 1, :] = jnp.sum(found, axis=0, keepdims=True).astype(I32)
    copy = pltpu.make_async_copy(out_ref, slots, sem)
    copy.start()
    copy.wait()


def fetch_kernel(side_of, a_hbm, cot, a_side, c0, c1, c2, c3, sems):
    _, c, x = position()
    pieces = (c0, c1, c2, c3)
    width = c0.shape[1]
    copies = []
    for q in (1, 2, 3, 0):
        at = rows_at((c ^ (q & 1)) * 2 + (x ^ (q >> 1)), width)
        copies.append(pltpu.make_async_copy(cot.at[:, at], pieces[q], sems.at[q]))
    n = a_side.shape[0]
    first = (2 * c + side_of(x)) * n
    for i in range(n):
        copies.append(pltpu.make_async_copy(a_hbm.at[first + i], a_side.at[i], sems.at[4 + i]))
    for copy in copies:
        copy.start()
    for copy in copies:
        copy.wait()


def gather(side_of, slot, a_side, mine, mate, got, got_mate, out, table):
    r, c, x = position()
    f = mine.shape[0]
    top, low = rows_at(c, f), rows_at(1 - c, f)
    n, slots_n, tile, _ = a_side.shape
    blk = mine.shape[1] // tile
    for b in range(blk):
        table[b, top, :] = mine[:, b * tile : (b + 1) * tile]
        table[b, low, :] = mate[:, b * tile : (b + 1) * tile]
    for d in range(got.shape[0]):
        for o in range(CAP):
            table[blk + d * CAP + o, top, :] = got[d, o]
            table[blk + d * CAP + o, low, :] = got_mate[d, o]
    lane = lax.rem(r * 4 * n, LANES) + (2 * c + side_of(x)) * n
    for t in range(n):
        acc = None
        for k in range(0, slots_n, 2):
            left = [table[slot[k + h, lane + t]] for h in range(2)]
            right = [a_side[t, k + h] for h in range(2)]
            part = lax.dot_general(
                jnp.concatenate(right, axis=1),
                jnp.concatenate(left, axis=1),
                (((1,), (1,)), ((), ())),
                preferred_element_type=F32,
            )
            acc = part if acc is None else acc + part
        out[:, t * tile : (t + 1) * tile] = acc.T.astype(BF16)


def fetch_near_kernel(side_of, a_hbm, a_side, sems):
    _, c, x = position()
    n = a_side.shape[0]
    first = (2 * c + side_of(x)) * n
    copies = []
    for i in range(n):
        copies.append(pltpu.make_async_copy(a_hbm.at[first + i], a_side.at[i], sems.at[i]))
        copies[-1].start()
    for copy in copies:
        copy.wait()


def dense_kernel(keep, came, w_ref, c0, c1, c2, c3, *rest):
    outs, (g_send, g_keep, wg_send, wg_keep) = rest[:4], rest[4:8]
    agg, cot, out_s, grad_s, wg_s = rest[8:]
    _, c, x = position()
    fx = keep.shape[0]
    u = c0.shape[0]
    col = 2 * x + c
    agg[rows_at(x, fx), :] = keep[...]
    agg[rows_at(1 - x, fx), :] = came[...]
    for q, piece in enumerate((c0, c1, c2, c3)):
        cot[rows_at(col ^ q, u), :] = piece[...]
    w = w_ref[...]
    act = agg[...]
    pre_act = lax.dot_general(w, act, (((0,), (0,)), ((), ())), preferred_element_type=F32)
    sigm = jax.nn.sigmoid(pre_act)
    out_s[...] = (pre_act * sigm).astype(BF16)
    pre = (cot[...].astype(F32) * sigm * (1.0 + pre_act * (1.0 - sigm))).astype(BF16)
    grad_s[...] = jnp.dot(w, pre, preferred_element_type=F32).astype(BF16)
    wg_s[...] = lax.dot_general(act, pre, (((1,), (1,)), ((), ())), preferred_element_type=F32)
    g_keep[...] = grad_s[rows_at(x, fx), :]
    g_send[...] = grad_s[rows_at(1 - x, fx), :]
    f = fx // 2
    for h in range(2):
        wg_keep[h * f : (h + 1) * f, :] = wg_s[rows_at(2 * h + c, f), :]
        wg_send[h * f : (h + 1) * f, :] = wg_s[rows_at(2 * h + 1 - c, f), :]
    for q in range(4):
        outs[q][...] = out_s[rows_at(col ^ q, u), :]


def wg_kernel(mine, came, keep, send):
    _, _, x = position()
    f = keep.shape[0]
    keep[...] = mine[rows_at(x, f), :] + came[rows_at(x, f), :]
    send[...] = mine[rows_at(1 - x, f), :] + came[rows_at(1 - x, f), :]


def spread(side_of, slot, a_side, g_ref, acc):
    r, c, x = position()
    n, slots_n, tile, _ = a_side.shape
    lane = lax.rem(r * 4 * n, LANES) + (2 * c + side_of(x)) * n
    for t in range(n):
        g = g_ref[:, t * tile : (t + 1) * tile]
        for k in range(0, slots_n, 2):
            right = jnp.concatenate([a_side[t, k], a_side[t, k + 1]], axis=1)
            part = jnp.dot(g, right, preferred_element_type=F32)
            acc[slot[k, lane + t]] += part[:, :tile]
            acc[slot[k + 1, lane + t]] += part[:, tile:]


def spread_first_kernel(side_of, slot, a_side, g_ref, acc):
    acc[...] = jnp.zeros_like(acc)
    spread(side_of, slot, a_side, g_ref, acc)


def spread_last_kernel(side_of, out_order, back_order, slot, a_side, g_ref, before, own, own_send, stay, send, acc):
    acc[...] = before[...]
    spread(side_of, slot, a_side, g_ref, acc)
    _, c, _ = position()
    f = own.shape[0]
    top, low = rows_at(c, f), rows_at(1 - c, f)
    tile = a_side.shape[3]
    blk = own.shape[1] // tile
    for p, d in enumerate(back_order):
        at = blk + out_order.index(d) * CAP
        for o in range(CAP):
            stay[p, o] = acc[at + o, top, :]
            send[p, o] = acc[at + o, low, :].astype(BF16)
    for b in range(blk):
        own[:, b * tile : (b + 1) * tile] = acc[b, top, :]
        own_send[:, b * tile : (b + 1) * tile] = acc[b, low, :]


def total_kernel(stay, came, wg, wg_came, out, packed, sems):
    f, tile = stay.shape[2], stay.shape[3]
    part = (wg[...] + wg_came[...]).astype(BF16)
    copies = []
    for d in range(stay.shape[0]):
        for o in range(CAP):
            packed[d, o * f : (o + 1) * f, :] = (stay[d, o] + came[d, o].astype(F32)).astype(BF16)
        for h in range(part.shape[1] // tile):
            at = (CAP + h) * f
            packed[d, at : at + f, :] = part[:, h * tile : (h + 1) * tile]
        copies.append(pltpu.make_async_copy(packed.at[d], out.at[d], sems.at[d]))
        copies[-1].start()
    for copy in copies:
        copy.wait()


def collect_kernel(scale, back_order, sel, own, came, back, out, wg_out, acc, wg, sems):
    tile = back.shape[2]
    f = own.shape[0]
    half = f // 2
    copies = []
    for h in range(2):
        rows = slice(h * half, (h + 1) * half)
        acc[rows, :] = own[rows, :] + came[rows, :]
        for p, d in enumerate(back_order):
            for o in range(CAP):
                term = back[p, o * f + h * half : o * f + (h + 1) * half, :].astype(F32)
                acc[rows, rows_at(sel[o, d], tile)] += term
        copies.append(pltpu.make_async_copy(acc.at[rows, :], out.at[rows, :], sems.at[h]))
        copies[-1].start()
    for h in range(wg.shape[1] // tile):
        at = (CAP + h) * f
        total = back[0, at : at + f, :].astype(F32)
        for d in range(1, back.shape[0]):
            total = total + back[d, at : at + f, :].astype(F32)
        wg[:, h * tile : (h + 1) * tile] = total * scale
    copies.append(pltpu.make_async_copy(wg, wg_out, sems.at[2]))
    copies[-1].start()
    for copy in copies:
        copy.wait()


def place_kernel(p0, p1, p2, p3, out):
    _, c, x = position()
    width = p0.shape[1]
    for q, piece in enumerate((p0, p1, p2, p3)):
        out[:, rows_at((c ^ (q & 1)) * 2 + (x ^ (q >> 1)), width)] = piece[...]


def layer(feats_t, adj_index, adj_weight, weight, cotangent_t):
    f, nodes = feats_t.shape
    blk, slots_n, tile, _ = adj_weight.shape
    units_loc = cotangent_t.shape[0]
    f_in, units = weight.shape
    rows_n, cols_n = lax.axis_size("rows"), lax.axis_size("cols")
    assert cols_n == 4 and rows_n & (rows_n - 1) == 0 and blk % 4 == 0
    table_n = blk + rows_n * CAP
    fx = 2 * f
    quarter = nodes // 4
    big = min(48, 8 + rows_n)

    def mate(v, q):
        return lax.ppermute(v, "cols", [(i, i ^ q) for i in range(cols_n)])

    out_order, back_order = order_of(rows_n), back_order_of(rows_n)

    def over_rows(v, order):
        return lax.all_to_all(v, "rows", 0, 0, tiled=True, axis_index_groups=[order])

    adj_t = adj_index.T
    in_hbm = functools.partial(pltpu.with_memory_space_constraint, memory_space=pltpu.HBM)
    part = (rows_n, CAP, f, tile)
    piece = ("vmem", (units_loc, quarter), BF16)
    sel, feats, adj, sends = call(
        functools.partial(choose_kernel, out_order), [HBM, HBM],
        [("smem", (CAP, rows_n), I32), ("vmem", (f, nodes), BF16), ("vmem", adj_t.shape, I32),
         ("hbm", part, BF16)],
        [in_hbm(adj_t), in_hbm(feats_t)], [pltpu.SemaphoreType.DMA((3,))], mib=big,
    )
    feats_mate = mate(feats, 1)
    got = over_rows(sends, out_order)

    def far(x):
        return 1 - x

    def near(x):
        return x

    a_side = ("vmem", (blk // 4, slots_n, tile, tile), BF16)
    sems = [pltpu.SemaphoreType.DMA((4 + blk // 4,))]
    a_far, *cots = call(
        functools.partial(fetch_kernel, far), [HBM, HBM], [a_side] + [piece] * 4,
        [in_hbm(adj_weight), in_hbm(cotangent_t)], sems,
    )
    slot = call(
        functools.partial(slot_kernel, out_order, blk), [VMEM],
        [("smem", (slots_n, LANES), I32)], [adj],
        [pltpu.VMEM((slots_n, LANES), I32), pltpu.SemaphoreType.DMA], mib=big,
    )
    cots = [cots[0]] + [mate(cots[q], q) for q in (1, 2, 3)]
    got_mate = mate(got, 1)

    a_flops = blk // 2 * slots_n * fx * tile * tile

    half_g = ("vmem", (fx, quarter), BF16)

    tables = [feats, feats_mate, got, got_mate]
    table = pltpu.VMEM((table_n, fx, tile), BF16)
    agg_far = call(
        functools.partial(gather, far), [SMEM] + [VMEM] * 5, [half_g],
        [slot, a_far, *tables], [table], a_flops, big,
    )
    agg_came = mate(agg_far, 2)
    a_near = call(
        functools.partial(fetch_near_kernel, near), [HBM], [a_side],
        [in_hbm(adj_weight)], [pltpu.SemaphoreType.DMA((blk // 4,))],
    )
    agg_near = call(
        functools.partial(gather, near), [SMEM] + [VMEM] * 5, [half_g],
        [slot, a_near, *tables], [table], a_flops, big,
    )

    args = [agg_near, agg_came, weight, *cots]
    *outs, g_send, g_keep, wg_send, wg_keep = call(
        dense_kernel, [VMEM] * len(args),
        [piece] * 4 + [half_g] * 2 + [("vmem", (fx, units), F32)] * 2, args,
        [
            pltpu.VMEM((f_in, quarter), BF16),
            pltpu.VMEM((units, quarter), BF16),
            pltpu.VMEM((units, quarter), BF16),
            pltpu.VMEM((f_in, quarter), BF16),
            pltpu.VMEM((f_in, units), F32),
        ],
        6 * f_in * units * quarter, 12,
    )
    g_came = mate(g_send, 2)
    wg_part = ((f, units), F32)
    wg_keep, wg_send = call(
        wg_kernel, [VMEM] * 2, [("vmem", *wg_part)] * 2, [wg_keep, mate(wg_send, 1)]
    )
    wg_came = mate(wg_send, 2)

    acc = call(
        functools.partial(spread_first_kernel, near), [SMEM, VMEM, VMEM],
        [("vmem", (table_n, fx, tile), F32)], [slot, a_near, g_keep], [], a_flops, big,
    )
    own, own_send, stay, send = call(
        functools.partial(spread_last_kernel, far, out_order, back_order), [SMEM] + [VMEM] * 3,
        [("vmem", (f, nodes), F32)] * 2 + [("vmem", part, F32), ("vmem", part, BF16)],
        [slot, a_far, g_came, acc], [pltpu.VMEM((table_n, fx, tile), F32)], a_flops, big + 8,
    )
    packed = ((rows_n, CAP * f + f * units // tile, tile), BF16)
    total = call(
        total_kernel, [VMEM] * 4, [("hbm", *packed)],
        [stay, mate(send, 1), wg_keep, wg_came],
        [pltpu.VMEM(*packed), pltpu.SemaphoreType.DMA((rows_n,))], mib=big,
    )
    back = over_rows(total, back_order)
    own_came = mate(own_send, 1)
    feat_grad, weight_grad = call(
        functools.partial(collect_kernel, 1.0 / math.sqrt(nodes * rows_n), back_order),
        [SMEM, VMEM, VMEM, VMEM], [("hbm", (f, nodes), F32), ("hbm", *wg_part)],
        [sel, own, own_came, back],
        [pltpu.VMEM((f, nodes), F32), pltpu.VMEM(*wg_part), pltpu.SemaphoreType.DMA((3,))],
        mib=big,
    )

    outs = [outs[0]] + [mate(outs[q], q) for q in (1, 2, 3)]
    output_t = call(place_kernel, [VMEM] * 4, [("out", (units_loc, nodes), BF16)], outs)
    return output_t, weight_grad, feat_grad


def solution(mesh):
    return jax.shard_map(
        layer,
        mesh=mesh,
        in_specs=(P("cols", "rows"), P(), P("rows", None, None, None), P(), P("cols", "rows")),
        out_specs=(P("cols", "rows"), P("cols", None), P("cols", "rows")),
        check_vma=False,
    )
```

```python
import functools
import math

import jax
import jax.numpy as jnp
from jax import lax
from jax.experimental import pallas as pl
from jax.experimental.pallas import tpu as pltpu
from jax.sharding import PartitionSpec as P

CAP = 4
LANES = 128
F32, BF16, I32 = jnp.float32, jnp.bfloat16, jnp.int32
VMEM = pl.BlockSpec(memory_space=pltpu.VMEM)
SMEM = pl.BlockSpec(memory_space=pltpu.SMEM)
HBM = pl.BlockSpec(memory_space=pltpu.HBM)
MIB = 1 << 20
BACK_ORDERS = {8: (4, 1, 3, 6, 2, 0, 5, 7)}


def order_of(rows_n):
    bits = (rows_n // 2).bit_length() - 1
    order = []
    for i in range(rows_n // 2):
        gray = i ^ (i >> 1)
        at = sum(((gray >> b) & 1) << (bits - 1 - b) for b in range(bits)) + rows_n // 2
        order += [at, rows_n - 1 - at]
    return order


def back_order_of(rows_n):
    if rows_n in BACK_ORDERS:
        return list(BACK_ORDERS[rows_n])
    pairs = rows_n // 2
    middle = [*range(pairs // 2, pairs), *range(pairs // 2 - 1, -1, -1)]
    return [2 * i for i in middle] + [2 * i + 1 for i in middle]


def call(kernel, in_specs, outs, args, scratch=(), flops=10**6, mib=8):
    kinds = {"vmem": (pltpu.VMEM, VMEM), "smem": (pltpu.SMEM, SMEM)}
    shapes = [kinds[k][0](s, d) if k in kinds else jax.ShapeDtypeStruct(s, d) for k, s, d in outs]
    specs = [kinds[k][1] if k in kinds else {"hbm": HBM, "out": VMEM}[k] for k, _, _ in outs]
    nbytes = sum(a.size * a.dtype.itemsize for a in args)
    result = pl.pallas_call(
        kernel,
        out_shape=shapes,
        in_specs=in_specs,
        out_specs=specs,
        scratch_shapes=list(scratch),
        compiler_params=pltpu.CompilerParams(vmem_limit_bytes=mib * MIB),
        cost_estimate=pl.CostEstimate(flops=flops, bytes_accessed=nbytes, transcendentals=0),
    )(*args)
    return result if len(outs) > 1 else result[0]


def iota(shape, dim):
    return lax.broadcasted_iota(I32, shape, dim)


def position():
    col = lax.axis_index("cols")
    return lax.axis_index("rows"), lax.rem(col, 2), col // 2


def rows_at(start, size):
    return pl.ds(pl.multiple_of(start * size, size), size)


def choose_kernel(order, adj_hbm, feats, sel, copied, adj_ref, sends, sems):
    names = pltpu.make_async_copy(adj_hbm, adj_ref, sems.at[0])
    names.start()
    copy = pltpu.make_async_copy(feats, copied, sems.at[1])
    copy.start()
    slots_n, ids_n = adj_ref.shape
    tile = sends.shape[3]
    blk = feats.shape[1] // tile
    r, _, _ = position()
    mine = r * blk + iota((blk, ids_n), 0)
    group = (iota((ids_n, LANES), 0) // blk == iota((ids_n, LANES), 1)).astype(BF16)
    below = (iota((blk, blk), 1) < iota((blk, blk), 0)).astype(BF16)
    number = iota((blk, LANES), 0).astype(F32)
    names.wait()
    adj = adj_ref[...]
    hits = jnp.zeros((blk, ids_n), F32)
    for k in range(slots_n):
        hits += (adj[k : k + 1, :] == mine).astype(F32)
    wants = jnp.dot(hits.astype(BF16), group, preferred_element_type=F32) > 0.5
    rank = jnp.dot(below, wants.astype(BF16), preferred_element_type=F32)
    picks = []
    for o in range(CAP):
        pick = jnp.where(wants & (jnp.abs(rank - o) < 0.5), number, 0.0)
        picks.append(jnp.sum(pick, axis=0, keepdims=True).astype(I32))
    copy.wait()
    for p, d in enumerate(order):
        for o in range(CAP):
            at = picks[o][0, d]
            sel[o, d] = at
            source = copied.at[:, rows_at(at, tile)]
            pltpu.make_async_copy(source, sends.at[p, o], sems.at[2]).start()
    pltpu.make_async_copy(sends, sends, sems.at[2]).wait()


def slot_kernel(order, blk, adj_ref, slots, out_ref, sem):
    slots_n, ids_n = adj_ref.shape
    r, _, _ = position()
    start = pl.multiple_of((r * blk) // LANES * LANES, LANES)
    near = adj_ref[:, pl.ds(start, LANES)]
    block = iota((ids_n, LANES), 0)
    seen = jnp.zeros((ids_n, LANES), F32)
    for k in range(slots_n):
        seen += (near[k : k + 1, :] == block).astype(F32)
    own = ((iota((LANES, LANES), 0) + start) // blk == r).astype(BF16)
    needed = jnp.dot(seen.astype(BF16), own, preferred_element_type=F32) > 0.5
    a, b = iota((ids_n, ids_n), 0), iota((ids_n, ids_n), 1)
    earlier = ((b < a) & (a // blk == b // blk)).astype(BF16)
    place = jnp.dot(earlier, needed.astype(BF16), preferred_element_type=F32).astype(I32)
    turn = [jnp.full((blk, LANES), order.index(d), I32) for d in range(len(order))]
    remote = blk + jnp.concatenate(turn, axis=0) * CAP + place
    slot = jnp.where(block // blk == r, block % blk, remote).astype(F32)
    for k in range(slots_n):
        found = jnp.where(near[k : k + 1, :] == block, slot, 0.0)
        out_ref[k : k + 1, :] = jnp.sum(found, axis=0, keepdims=True).astype(I32)
    copy = pltpu.make_async_copy(out_ref, slots, sem)
    copy.start()
    copy.wait()


def fetch_kernel(side_of, a_hbm, cot, a_side, c0, c1, c2, c3, sems):
    _, c, x = position()
    pieces = (c0, c1, c2, c3)
    width = c0.shape[1]
    copies = []
    for q in (1, 2, 3, 0):
        at = rows_at((c ^ (q & 1)) * 2 + (x ^ (q >> 1)), width)
        copies.append(pltpu.make_async_copy(cot.at[:, at], pieces[q], sems.at[q]))
    n = a_side.shape[0]
    first = (2 * c + side_of(x)) * n
    for i in range(n):
        copies.append(pltpu.make_async_copy(a_hbm.at[first + i], a_side.at[i], sems.at[4 + i]))
    for copy in copies:
        copy.start()
    for copy in copies:
        copy.wait()


def gather(side_of, slot, a_side, mine, mate, got, got_mate, out, table):
    r, c, x = position()
    f = mine.shape[0]
    top, low = rows_at(c, f), rows_at(1 - c, f)
    n, slots_n, tile, _ = a_side.shape
    blk = mine.shape[1] // tile
    for b in range(blk):
        table[b, top, :] = mine[:, b * tile : (b + 1) * tile]
        table[b, low, :] = mate[:, b * tile : (b + 1) * tile]
    for d in range(got.shape[0]):
        for o in range(CAP):
            table[blk + d * CAP + o, top, :] = got[d, o]
            table[blk + d * CAP + o, low, :] = got_mate[d, o]
    lane = lax.rem(r * 4 * n, LANES) + (2 * c + side_of(x)) * n
    for t in range(n):
        acc = None
        for k in range(0, slots_n, 2):
            left = [table[slot[k + h, lane + t]] for h in range(2)]
            right = [a_side[t, k + h] for h in range(2)]
            part = lax.dot_general(
                jnp.concatenate(left, axis=1),
                jnp.concatenate(right, axis=1),
                (((1,), (1,)), ((), ())),
                preferred_element_type=F32,
            )
            acc = part if acc is None else acc + part
        out[:, t * tile : (t + 1) * tile] = acc.astype(BF16)


def fetch_near_kernel(side_of, a_hbm, a_side, sems):
    _, c, x = position()
    n = a_side.shape[0]
    first = (2 * c + side_of(x)) * n
    copies = []
    for i in range(n):
        copies.append(pltpu.make_async_copy(a_hbm.at[first + i], a_side.at[i], sems.at[i]))
        copies[-1].start()
    for copy in copies:
        copy.wait()


def dense_kernel(keep, came, w_ref, c0, c1, c2, c3, *rest):
    outs, (g_send, g_keep, wg_send, wg_keep) = rest[:4], rest[4:8]
    agg, cot, out_s, grad_s, wg_s = rest[8:]
    _, c, x = position()
    fx = keep.shape[0]
    u = c0.shape[0]
    col = 2 * x + c
    agg[rows_at(x, fx), :] = keep[...]
    agg[rows_at(1 - x, fx), :] = came[...]
    for q, piece in enumerate((c0, c1, c2, c3)):
        cot[rows_at(col ^ q, u), :] = piece[...]
    w = w_ref[...]
    act = agg[...]
    pre_act = lax.dot_general(w, act, (((0,), (0,)), ((), ())), preferred_element_type=F32)
    sigm = jax.nn.sigmoid(pre_act)
    out_s[...] = (pre_act * sigm).astype(BF16)
    pre = (cot[...].astype(F32) * sigm * (1.0 + pre_act * (1.0 - sigm))).astype(BF16)
    grad_s[...] = jnp.dot(w, pre, preferred_element_type=F32).astype(BF16)
    wg_s[...] = lax.dot_general(act, pre, (((1,), (1,)), ((), ())), preferred_element_type=F32)
    g_keep[...] = grad_s[rows_at(x, fx), :]
    g_send[...] = grad_s[rows_at(1 - x, fx), :]
    f = fx // 2
    for h in range(2):
        wg_keep[h * f : (h + 1) * f, :] = wg_s[rows_at(2 * h + c, f), :]
        wg_send[h * f : (h + 1) * f, :] = wg_s[rows_at(2 * h + 1 - c, f), :]
    for q in range(4):
        outs[q][...] = out_s[rows_at(col ^ q, u), :]


def wg_kernel(mine, came, keep, send):
    _, _, x = position()
    f = keep.shape[0]
    keep[...] = mine[rows_at(x, f), :] + came[rows_at(x, f), :]
    send[...] = (mine[rows_at(1 - x, f), :] + came[rows_at(1 - x, f), :]).astype(BF16)


def spread(side_of, slot, a_side, g_ref, acc):
    r, c, x = position()
    n, slots_n, tile, _ = a_side.shape
    lane = lax.rem(r * 4 * n, LANES) + (2 * c + side_of(x)) * n
    for t in range(n):
        g = g_ref[:, t * tile : (t + 1) * tile]
        for k in range(0, slots_n, 2):
            right = jnp.concatenate([a_side[t, k], a_side[t, k + 1]], axis=1)
            part = jnp.dot(g, right, preferred_element_type=F32)
            acc[slot[k, lane + t]] += part[:, :tile]
            acc[slot[k + 1, lane + t]] += part[:, tile:]


def spread_first_kernel(side_of, slot, a_side, g_ref, acc):
    acc[...] = jnp.zeros_like(acc)
    spread(side_of, slot, a_side, g_ref, acc)


def spread_last_kernel(side_of, out_order, back_order, slot, a_side, g_ref, before, own, own_send, stay, send, acc):
    acc[...] = before[...]
    spread(side_of, slot, a_side, g_ref, acc)
    _, c, _ = position()
    f = own.shape[0]
    top, low = rows_at(c, f), rows_at(1 - c, f)
    tile = a_side.shape[3]
    blk = own.shape[1] // tile
    for p, d in enumerate(back_order):
        at = blk + out_order.index(d) * CAP
        for o in range(CAP):
            stay[p, o] = acc[at + o, top, :]
            send[p, o] = acc[at + o, low, :].astype(BF16)
    for b in range(blk):
        own[:, b * tile : (b + 1) * tile] = acc[b, top, :]
        own_send[:, b * tile : (b + 1) * tile] = acc[b, low, :]


def total_kernel(stay, came, wg, wg_came, out, packed, sems):
    f, tile = stay.shape[2], stay.shape[3]
    part = (wg[...] + wg_came[...].astype(F32)).astype(BF16)
    copies = []
    for d in range(stay.shape[0]):
        for o in range(CAP):
            packed[d, o * f : (o + 1) * f, :] = (stay[d, o] + came[d, o].astype(F32)).astype(BF16)
        for h in range(part.shape[1] // tile):
            at = (CAP + h) * f
            packed[d, at : at + f, :] = part[:, h * tile : (h + 1) * tile]
        copies.append(pltpu.make_async_copy(packed.at[d], out.at[d], sems.at[d]))
        copies[-1].start()
    for copy in copies:
        copy.wait()


def collect_kernel(scale, back_order, sel, own, came, back, out, wg_out, acc, wg, sems):
    tile = back.shape[2]
    f = own.shape[0]
    half = f // 2
    copies = []
    for h in range(2):
        rows = slice(h * half, (h + 1) * half)
        acc[rows, :] = own[rows, :] + came[rows, :]
        for p, d in enumerate(back_order):
            for o in range(CAP):
                term = back[p, o * f + h * half : o * f + (h + 1) * half, :].astype(F32)
                acc[rows, rows_at(sel[o, d], tile)] += term
        copies.append(pltpu.make_async_copy(acc.at[rows, :], out.at[rows, :], sems.at[h]))
        copies[-1].start()
    for h in range(wg.shape[1] // tile):
        at = (CAP + h) * f
        total = back[0, at : at + f, :].astype(F32)
        for d in range(1, back.shape[0]):
            total = total + back[d, at : at + f, :].astype(F32)
        wg[:, h * tile : (h + 1) * tile] = total * scale
    copies.append(pltpu.make_async_copy(wg, wg_out, sems.at[2]))
    copies[-1].start()
    for copy in copies:
        copy.wait()


def place_kernel(p0, p1, p2, p3, out):
    _, c, x = position()
    width = p0.shape[1]
    for q, piece in enumerate((p0, p1, p2, p3)):
        out[:, rows_at((c ^ (q & 1)) * 2 + (x ^ (q >> 1)), width)] = piece[...]


def layer(feats_t, adj_index, adj_weight, weight, cotangent_t):
    f, nodes = feats_t.shape
    blk, slots_n, tile, _ = adj_weight.shape
    units_loc = cotangent_t.shape[0]
    f_in, units = weight.shape
    rows_n, cols_n = lax.axis_size("rows"), lax.axis_size("cols")
    assert cols_n == 4 and rows_n & (rows_n - 1) == 0 and blk % 4 == 0
    table_n = blk + rows_n * CAP
    fx = 2 * f
    quarter = nodes // 4
    big = min(48, 8 + rows_n)

    def mate(v, q):
        return lax.ppermute(v, "cols", [(i, i ^ q) for i in range(cols_n)])

    out_order, back_order = order_of(rows_n), back_order_of(rows_n)

    def over_rows(v, order):
        return lax.all_to_all(v, "rows", 0, 0, tiled=True, axis_index_groups=[order])

    adj_t = adj_index.T
    in_hbm = functools.partial(pltpu.with_memory_space_constraint, memory_space=pltpu.HBM)
    part = (rows_n, CAP, f, tile)
    piece = ("vmem", (units_loc, quarter), BF16)
    sel, feats, adj, sends = call(
        functools.partial(choose_kernel, out_order), [HBM, HBM],
        [("smem", (CAP, rows_n), I32), ("vmem", (f, nodes), BF16), ("vmem", adj_t.shape, I32),
         ("hbm", part, BF16)],
        [in_hbm(adj_t), in_hbm(feats_t)], [pltpu.SemaphoreType.DMA((3,))], mib=big,
    )
    feats_mate = mate(feats, 1)
    got = over_rows(sends, out_order)

    def far(x):
        return 1 - x

    def near(x):
        return x

    a_side = ("vmem", (blk // 4, slots_n, tile, tile), BF16)
    sems = [pltpu.SemaphoreType.DMA((4 + blk // 4,))]
    a_far, *cots = call(
        functools.partial(fetch_kernel, far), [HBM, HBM], [a_side] + [piece] * 4,
        [in_hbm(adj_weight), in_hbm(cotangent_t)], sems,
    )
    slot = call(
        functools.partial(slot_kernel, out_order, blk), [VMEM],
        [("smem", (slots_n, LANES), I32)], [adj],
        [pltpu.VMEM((slots_n, LANES), I32), pltpu.SemaphoreType.DMA], mib=big,
    )
    cots = [cots[0]] + [mate(cots[q], q) for q in (1, 2, 3)]
    got_mate = mate(got, 1)

    a_flops = blk // 2 * slots_n * fx * tile * tile

    half_g = ("vmem", (fx, quarter), BF16)

    tables = [feats, feats_mate, got, got_mate]
    table = pltpu.VMEM((table_n, fx, tile), BF16)
    agg_far = call(
        functools.partial(gather, far), [SMEM] + [VMEM] * 5, [half_g],
        [slot, a_far, *tables], [table], a_flops, big,
    )
    agg_came = mate(agg_far, 2)
    a_near = call(
        functools.partial(fetch_near_kernel, near), [HBM], [a_side],
        [in_hbm(adj_weight)], [pltpu.SemaphoreType.DMA((blk // 4,))],
    )
    agg_near = call(
        functools.partial(gather, near), [SMEM] + [VMEM] * 5, [half_g],
        [slot, a_near, *tables], [table], a_flops, big,
    )

    args = [agg_near, agg_came, weight, *cots]
    *outs, g_send, g_keep, wg_send, wg_keep = call(
        dense_kernel, [VMEM] * len(args),
        [piece] * 4 + [half_g] * 2 + [("vmem", (fx, units), F32)] * 2, args,
        [
            pltpu.VMEM((f_in, quarter), BF16),
            pltpu.VMEM((units, quarter), BF16),
            pltpu.VMEM((units, quarter), BF16),
            pltpu.VMEM((f_in, quarter), BF16),
            pltpu.VMEM((f_in, units), F32),
        ],
        6 * f_in * units * quarter, 12,
    )
    g_came = mate(g_send, 2)
    wg_part = ((f, units), F32)
    wg_keep, wg_send = call(
        wg_kernel, [VMEM] * 2, [("vmem", *wg_part), ("vmem", wg_part[0], BF16)],
        [wg_keep, mate(wg_send, 1)],
    )
    wg_came = mate(wg_send, 2)

    acc = call(
        functools.partial(spread_first_kernel, near), [SMEM, VMEM, VMEM],
        [("vmem", (table_n, fx, tile), F32)], [slot, a_near, g_keep], [], a_flops, big,
    )
    own, own_send, stay, send = call(
        functools.partial(spread_last_kernel, far, out_order, back_order), [SMEM] + [VMEM] * 3,
        [("vmem", (f, nodes), F32)] * 2 + [("vmem", part, F32), ("vmem", part, BF16)],
        [slot, a_far, g_came, acc], [pltpu.VMEM((table_n, fx, tile), F32)], a_flops, big + 8,
    )
    packed = ((rows_n, CAP * f + f * units // tile, tile), BF16)
    total = call(
        total_kernel, [VMEM] * 4, [("hbm", *packed)],
        [stay, mate(send, 1), wg_keep, wg_came],
        [pltpu.VMEM(*packed), pltpu.SemaphoreType.DMA((rows_n,))], mib=big,
    )
    back = over_rows(total, back_order)
    own_came = mate(own_send, 1)
    feat_grad, weight_grad = call(
        functools.partial(collect_kernel, 1.0 / math.sqrt(nodes * rows_n), back_order),
        [SMEM, VMEM, VMEM, VMEM], [("hbm", (f, nodes), F32), ("hbm", *wg_part)],
        [sel, own, own_came, back],
        [pltpu.VMEM((f, nodes), F32), pltpu.VMEM(*wg_part), pltpu.SemaphoreType.DMA((3,))],
        mib=big,
    )

    outs = [outs[0]] + [mate(outs[q], q) for q in (1, 2, 3)]
    output_t = call(place_kernel, [VMEM] * 4, [("out", (units_loc, nodes), BF16)], outs)
    return output_t, weight_grad, feat_grad


def solution(mesh):
    return jax.shard_map(
        layer,
        mesh=mesh,
        in_specs=(P("cols", "rows"), P(), P("rows", None, None, None), P(), P("cols", "rows")),
        out_specs=(P("cols", "rows"), P("cols", None), P("cols", "rows")),
        check_vma=False,
    )
```
